256 devices in a mesh: edge: 16 (over x, y), tile: 16 (over z, core).
Axes of the slice: x: 4, y: 4, z: 8, core: 2. Of those that a mesh axis runs over, the one named last changes fastest.
Arguments:
- features: bfloat16 [384, 48, 64, 128], P('edge', 'tile'), may hold values from -6 to 6
- hidden_state: bfloat16 [128, 48, 64, 128], P('edge', 'tile'), may hold values from -1 to 1
- edge_source: int32 [128], P('edge'), may hold values from 0 to 23
- edge_owner: int32 [128, 1], P('edge'), may hold values from 0 to 15; in each aligned block of 8 rows (0 to 7, 8 to 15, ...) at most 2 rows name the same one
- edge_target: int32 [128], P('edge'), may hold values from 0 to 23
- edge_counts: int32 [16], P('edge'), may hold values from 4 to 8, as said below
- corr_weight: bfloat16 [49, 128], replicated, may hold values from -0.875 to 0.875
- gate_weight: bfloat16 [3, 3, 256, 256], replicated, may hold values from -0.125 to 0.125
- candidate_weight: bfloat16 [3, 3, 256, 128], replicated, may hold values from -0.125 to 0.125
- jacobian_weight: bfloat16 [128, 24], replicated, may hold values from -0.5 to 0.5
- confidence_weight: bfloat16 [128, 2], replicated, may hold values from -3 to 3
Outputs:
- hidden_next: bfloat16 [128, 48, 64, 128], P('edge', 'tile')
- camera_hessian: float32 [2304, 2304], P('tile', 'edge')
- pose_diagonal: float32 [384, 36], P('edge')
The draws below stay inside these ranges and needn't reach their ends.
Inputs may be any that keep to these rules, and one draw needn't show every extreme that they name: `edge_owner`: in the rows of one index of edge at most 2 edges name the same owner, a bound that some block reaches. `edge_counts`: edges past a device's count are unused; some index of edge uses all 8.
All inputs are finite; a program needn't handle non-finite values.
Results may differ from the reference program's by a relative error of at most 0.015.
Values may be sent and summed in bfloat16 or wider, within the bound.
No kernel may reach another device: no remote copies, remote signals or barrier semaphores. Data moves between devices by JAX's collectives and lax.ppermute only.
A program may use at most 128 MiB of HBM per device.

```python
import math
import jax
import jax.numpy as jnp
import numpy as np
from jax import lax

MAPH = 48
MAPW = 64
CH = 128
HID = 128
WINDOW = 7
FRAMES_DEV = 24
EDGES_DEV = 8
MOST = 2
FRAMES = 384
EDGES = 128
N_EDGE = 16


def draw_edge_counts(key, part):
    devices = EDGES // EDGES_DEV
    first_key, second_key = jax.random.split(jax.random.fold_in(key, 17))
    counts = jax.random.randint(first_key, (devices,), EDGES_DEV // 2, EDGES_DEV + 1)
    fullest = jax.random.randint(second_key, (), 0, devices)
    return jnp.where(jnp.arange(devices) == fullest, EDGES_DEV, counts).astype(jnp.int32)


def plant(entries, key, least, top_value):
    spot = [jax.random.randint(jax.random.fold_in(key, axis), (), 0, length) for axis, length in enumerate(entries.shape)]
    main_axis = entries.shape.index(max(entries.shape))
    beside = spot[:main_axis] + [(spot[main_axis] + 1) % entries.shape[main_axis]] + spot[main_axis + 1:]
    return entries.at[tuple(spot)].set(least).at[tuple(beside)].set(top_value)


def block_levels(rng, extent, shards, low, top_value):
    factor_of = 1.0
    for position, shards_of in shards:
        draws = jax.random.uniform(jax.random.fold_in(jax.random.fold_in(rng, 6), position), (shards_of,), jnp.float32, low / len(shards), top_value / len(shards))
        factor_of = factor_of * jnp.repeat(jnp.exp(draws), extent[position] // shards_of).reshape((-1,) + (1,) * (len(extent) - 1 - position))
    return factor_of


def routed_block(rng, own, number, rows, amount, top, reach, lean):
    ranking = jax.random.permutation(rng, amount)
    crowded, usual = shares(amount, rows * top, reach, lean, True), shares(amount, rows * top, reach, lean, False)
    places = jnp.arange(amount)

    def named(lengths, rotation):
        used = int((lengths > 0).sum())
        fixed = max(1, used // 4)
        passed = fixed + (places - fixed + rotation * (used - fixed)) % max(1, amount - fixed)
        return jnp.zeros((amount,), jnp.int32).at[ranking[jnp.where(places < fixed, places, passed)]].set(jnp.asarray(lengths, jnp.int32))

    lengths = jnp.where(number % 4 == 0, named(crowded, number // 4), named(usual, number - number // 4 - 1))
    mixed = jax.random.permutation(jax.random.fold_in(own, 3), amount)
    source_of, taker = mixed[0:amount // 2 * 2:2], mixed[1:amount // 2 * 2:2]
    margin = jnp.minimum(lengths[source_of] - 1, reach - lengths[taker]) // 2
    margin = jnp.where((source_of == ranking[0]) | (taker == ranking[0]) | (lengths[taker] == 0), 0, jnp.maximum(margin, 0))
    passed = jax.random.randint(jax.random.fold_in(own, 4), (amount // 2,), 0, 1 << 20) % (margin + 1)
    lengths = lengths.at[source_of].add(-passed).at[taker].add(passed)
    labels = jnp.searchsorted(jnp.cumsum(lengths), jnp.arange(rows * top), side="right").astype(jnp.int32)
    table = labels.reshape(top, rows).T
    table = table[jax.random.permutation(jax.random.fold_in(own, 1), rows)]
    rotation = jax.random.randint(jax.random.fold_in(own, 2), (rows, 1), 0, top)
    return jnp.take_along_axis(table, (jnp.arange(top)[None, :] + rotation) % top, axis=1)


def shares(count, total, bound, slope, full):
    loads = [(1 << 20) // math.isqrt(standing ** slope) + 1 for standing in range(1, count + 1)]
    largest = bound if full else min(bound, max(-(-total // count), total * loads[0] // sum(loads)))
    least = 1 if total - largest >= count - 1 else 0
    holding, surplus = [largest] + [least] * (count - 1), total - largest - least * (count - 1)
    while surplus > 0:
        candidates = [i for i in range(1, count) if holding[i] < largest] or [i for i in range(1, count) if holding[i] < bound]
        whole, left = sum([loads[i] for i in candidates]), surplus
        for i in candidates:
            more = min(bound - holding[i], max(1, left * loads[i] // whole), surplus)
            holding[i] = holding[i] + more
            surplus = surplus - more
    return np.array(holding)


def noise(own_key, dims, spread, most, shards=(), kind=jnp.bfloat16):
    loudness = block_levels(own_key, dims, shards, -0.22, 0.18) if shards else 1.0
    array = jax.random.normal(own_key, dims, jnp.float32) * spread * loudness
    return jnp.minimum(jnp.maximum(array, -most), most).astype(kind)


def setup_inputs(seed: int = 0) -> dict:
    seeds = jax.random.split(jax.random.key(seed), 12)
    features = noise(seeds[0], (FRAMES, MAPH, MAPW, CH), 1.0, 6.0, ((0, 16), (1, 16)))
    hidden_state = jnp.clip(jax.random.uniform(seeds[1], (EDGES, MAPH, MAPW, HID), jnp.float32, -1.0, 1.0) * block_levels(seeds[1], (EDGES, MAPH, MAPW, HID), ((0, 16), (1, 16)), -0.4, 0.0), -1.0, 1.0).astype(jnp.bfloat16)
    edge_source = plant(jax.random.randint(seeds[2], (EDGES,), 0, FRAMES_DEV), jax.random.fold_in(seeds[2], 1), 0, FRAMES_DEV - 1).astype(jnp.int32)
    edge_owner_keys = jax.random.split(jax.random.fold_in(seeds[3], 1), EDGES // EDGES_DEV)
    edge_owner_turns = jax.random.permutation(jax.random.fold_in(seeds[3], 3), EDGES // EDGES_DEV)
    edge_owner = jax.vmap(lambda own, number: routed_block(jax.random.fold_in(seeds[3], 2), own, number, EDGES_DEV, N_EDGE, 1, MOST, 1))(edge_owner_keys, edge_owner_turns).reshape((EDGES, 1))
    edge_target = plant(jax.random.randint(seeds[4], (EDGES,), 0, FRAMES_DEV), jax.random.fold_in(seeds[4], 1), 0, FRAMES_DEV - 1).astype(jnp.int32)
    edge_counts = draw_edge_counts(jax.random.fold_in(seeds[11], 71), 0)
    corr_weight = noise(seeds[6], (WINDOW * WINDOW, HID), (WINDOW * WINDOW) ** -0.5, 0.875)
    gate_weight = noise(seeds[7], (3, 3, 2 * HID, 2 * HID), (18 * HID) ** -0.5, 0.125)
    candidate_weight = noise(seeds[8], (3, 3, 2 * HID, HID), (18 * HID) ** -0.5, 0.125)
    jacobian_weight = noise(seeds[9], (HID, 24), HID ** -0.5, 0.5)
    confidence_weight = noise(seeds[10], (HID, 2), 0.5, 3.0)
    return dict(features=features, hidden_state=hidden_state, edge_source=edge_source, edge_owner=edge_owner, edge_target=edge_target, edge_counts=edge_counts, corr_weight=corr_weight, gate_weight=gate_weight, candidate_weight=candidate_weight, jacobian_weight=jacobian_weight, confidence_weight=confidence_weight)


def convolve(padded, weight):
    row_count = padded.shape[0] - 2
    col_count = padded.shape[1] - 2
    running = jnp.zeros((row_count, col_count, weight.shape[-1]), jnp.float32)
    for row_step in range(3):
        for col_step in range(3):
            window = padded[row_step:row_step + row_count, col_step:col_step + col_count].astype(jnp.float32)
            running = running + jnp.einsum('rwc,ck->rwk', window, weight[row_step, col_step].astype(jnp.float32))
    return running


def pad_map(values):
    return jnp.pad(values, ((1, 1), (1, 1), (0, 0)))


def window_corr(source_map, target_map):
    radius = WINDOW // 2
    padded = jnp.pad(target_map, ((radius, radius), (radius, radius), (0, 0)))
    columns = []
    for row_shift in range(WINDOW):
        for col_shift in range(WINDOW):
            moved = padded[row_shift:row_shift + MAPH, col_shift:col_shift + MAPW]
            columns.append(jnp.sum(source_map * moved, axis=-1))
    return jnp.stack(columns, axis=-1) * (CH ** -0.5)


def reference(features, hidden_state, edge_source, edge_owner, edge_target, edge_counts, corr_weight, gate_weight, candidate_weight, jacobian_weight, confidence_weight):
    edge_index = jnp.arange(EDGES, dtype=jnp.int32)
    device_of = edge_index // EDGES_DEV
    in_use = ((edge_index % EDGES_DEV) < edge_counts[device_of]).astype(jnp.float32)
    source_global = (device_of * FRAMES_DEV + edge_source).astype(jnp.int32)
    target_global = (edge_owner[:, 0] * FRAMES_DEV + edge_target).astype(jnp.int32)

    def edge_update(inputs):
        source_frame, target_frame, state, usage = inputs
        source_map = features[source_frame].astype(jnp.float32)
        target_map = features[target_frame].astype(jnp.float32)
        corr = window_corr(source_map, target_map).astype(jnp.bfloat16)
        motion = jax.nn.relu(jnp.einsum('rcd,dk->rck', corr.astype(jnp.float32), corr_weight.astype(jnp.float32))).astype(jnp.bfloat16)
        stacked = jnp.concatenate([state, motion], axis=-1)
        gates = jax.nn.sigmoid(convolve(pad_map(stacked), gate_weight))
        update = gates[..., :HID]
        reset = gates[..., HID:]
        state_float = state.astype(jnp.float32)
        reset_state = (reset * state_float).astype(jnp.bfloat16)
        mixed = jnp.concatenate([reset_state, motion], axis=-1)
        candidate = jnp.tanh(convolve(pad_map(mixed), candidate_weight))
        new_state = ((1.0 - update) * state_float + update * candidate).astype(jnp.bfloat16)
        new_float = new_state.astype(jnp.float32)
        jacobian = jnp.einsum('rwh,hk->krw', new_float, jacobian_weight.astype(jnp.float32)).reshape(2, 12, MAPH * MAPW)
        confidence = jax.nn.softplus(jnp.einsum('rwh,hk->krw', new_float, confidence_weight.astype(jnp.float32))).reshape(2, 1, MAPH * MAPW)
        normal_block = jnp.einsum('kap,kbp->ab', jacobian * confidence, jacobian, precision=lax.Precision.HIGHEST) / (MAPH * MAPW)
        normal_block = normal_block * usage
        kept = jnp.where(usage > 0, new_state, state)
        return kept, normal_block

    hidden_next, normal_blocks = lax.map(edge_update, (source_global, target_global, hidden_state, in_use))
    blocks4 = jnp.zeros((FRAMES, FRAMES, 6, 6), jnp.float32)
    blocks4 = blocks4.at[source_global, source_global].add(normal_blocks[:, :6, :6])
    blocks4 = blocks4.at[source_global, target_global].add(normal_blocks[:, :6, 6:])
    blocks4 = blocks4.at[target_global, source_global].add(normal_blocks[:, 6:, :6])
    blocks4 = blocks4.at[target_global, target_global].add(normal_blocks[:, 6:, 6:])
    frame_index = jnp.arange(FRAMES, dtype=jnp.int32)
    pose_diagonal = blocks4[frame_index, frame_index].reshape(FRAMES, 36)
    blocks4 = blocks4.at[frame_index, frame_index].set(jnp.zeros((FRAMES, 6, 6), jnp.float32))
    camera_hessian = blocks4.transpose(0, 2, 1, 3).reshape(6 * FRAMES, 6 * FRAMES)
    return hidden_next, camera_hessian, pose_diagonal
```

```python
import jax
import jax.numpy as jnp
from jax import lax
from jax.sharding import PartitionSpec as P

MAPH = 48
MAPW = 64
WINDOW = 7


def sent_together(arrays, axis, split_dim, concat_dim, along):
    widths = [a.shape[along] for a in arrays]
    both = jnp.concatenate(arrays, axis=along)
    filled = lax.all_to_all(both, axis, split_axis=split_dim, concat_axis=concat_dim, tiled=True)
    return tuple(jnp.split(filled, [sum(widths[:k]) for k in range(1, len(widths))], axis=along))


def padded_2(cells, sides, width):
    for axis, dim in sides:
        count = lax.axis_size(axis)
        place = lax.axis_index(axis)
        head = lax.slice_in_dim(cells, 0, width, axis=dim)
        tail = lax.slice_in_dim(cells, cells.shape[dim] - width, cells.shape[dim], axis=dim)
        above = lax.ppermute(tail, axis, [(i, (i + 1) % count) for i in range(count)])
        below = lax.ppermute(head, axis, [((i + 1) % count, i) for i in range(count)])
        cells = jnp.concatenate(
            [
                jnp.where(place == 0, jnp.zeros_like(above), above),
                cells,
                jnp.where(place == count - 1, jnp.zeros_like(below), below),
            ],
            axis=dim,
        )
    return cells


def total_of_pieces(shard, axis):
    count = lax.axis_size(axis)
    copies = jnp.broadcast_to(shard.reshape(1, shard.shape[0], -1), (count, shard.shape[0], shard.size // shard.shape[0]))
    parts = lax.all_to_all(copies, axis, split_axis=0, concat_axis=0, tiled=True)
    return parts.sum(axis=0).reshape(shard.shape)


def pad_columns(values):
    return jnp.pad(values, ((0, 0), (0, 0), (1, 1), (0, 0)))


def convolve(padded, weight):
    row_count = padded.shape[1] - 2
    col_count = padded.shape[2] - 2
    running = jnp.zeros((padded.shape[0], row_count, col_count, weight.shape[-1]), jnp.float32)
    for row_step in range(3):
        for col_step in range(3):
            window = padded[:, row_step : row_step + row_count, col_step : col_step + col_count]
            running = running + jnp.einsum(
                "erwc,ck->erwk",
                window,
                weight[row_step, col_step],
                preferred_element_type=jnp.float32,
            )
    return running


def per_device(
    features,
    hidden_state,
    edge_source,
    edge_owner,
    edge_target,
    edge_counts,
    corr_weight,
    gate_weight,
    candidate_weight,
    jacobian_weight,
    confidence_weight,
):
    edge_total = hidden_state.shape[0]
    frame_total = features.shape[0]
    band_rows = features.shape[1]
    map_width = features.shape[2]
    hidden_width = hidden_state.shape[3]
    owner_count = lax.axis_size("edge")
    slot_depth = max(2, (2 * edge_total + owner_count - 1) // owner_count)
    my_index = lax.axis_index("edge")
    in_use = jnp.arange(edge_total) < edge_counts[0]
    owners = edge_owner[:, 0]
    owner_hits = (owners[:, None] == jnp.arange(owner_count)[None, :]).astype(jnp.int32)
    earlier = jnp.cumsum(owner_hits, axis=0) - owner_hits
    rank_within = jnp.sum(earlier * owner_hits, axis=1)
    slot_index = owners * slot_depth + rank_within
    slot_hits = (slot_index[:, None] == jnp.arange(owner_count * slot_depth)[None, :]).astype(
        jnp.int32
    )
    source_global = my_index * frame_total + edge_source
    target_global = owners * frame_total + edge_target
    send_target = jnp.sum(slot_hits * edge_target[:, None], axis=0).reshape(owner_count, slot_depth)
    send_source = jnp.sum(slot_hits * source_global[:, None], axis=0).reshape(
        owner_count, slot_depth
    )
    got_target, got_source = sent_together((send_target, send_source), "edge", 0, 0, 1)
    asked = jnp.take(features, got_target.reshape(-1), axis=0, mode="clip").reshape(
        (owner_count, slot_depth) + features.shape[1:]
    )
    returned = lax.all_to_all(asked, "edge", split_axis=0, concat_axis=0, tiled=True)
    target_maps = jnp.take(
        returned.reshape((owner_count * slot_depth,) + features.shape[1:]), slot_index, axis=0, mode="clip"
    )
    radius = WINDOW // 2
    source_maps = jnp.take(features, edge_source, axis=0, mode="clip")
    target_rows = padded_2(target_maps, (("tile", 1),), radius)
    target_padded = jnp.pad(target_rows, ((0, 0), (0, 0), (radius, radius), (0, 0)))
    columns = []
    for row_shift in range(WINDOW):
        for col_shift in range(WINDOW):
            moved = target_padded[
                :, row_shift : row_shift + band_rows, col_shift : col_shift + map_width
            ]
            columns.append(
                jnp.einsum("erwh,erwh->erw", source_maps, moved, preferred_element_type=jnp.float32)
            )
    corr = (jnp.stack(columns, axis=-1) * features.shape[3] ** (-0.5)).astype(jnp.bfloat16)
    motion = jax.nn.relu(
        jnp.einsum("ercd,dk->erck", corr, corr_weight, preferred_element_type=jnp.float32)
    ).astype(jnp.bfloat16)
    stacked = jnp.concatenate([hidden_state, motion], axis=-1)
    state_float = hidden_state.astype(jnp.float32)
    extended = padded_2(stacked, (("tile", 1),), 2)
    gates = jax.nn.sigmoid(convolve(pad_columns(extended), gate_weight))
    inner = extended[:, 1:-1]
    reset_state = (
        gates[..., hidden_width:] * inner[..., :hidden_width].astype(jnp.float32)
    ).astype(jnp.bfloat16)
    mixed = jnp.concatenate([reset_state, inner[..., hidden_width:]], axis=-1)
    candidate = jnp.tanh(convolve(pad_columns(mixed), candidate_weight))
    update = gates[:, 1:-1, :, :hidden_width]
    new_state = ((1.0 - update) * state_float + update * candidate).astype(jnp.bfloat16)
    hidden_next = jnp.where(in_use[:, None, None, None], new_state, hidden_state)
    pixel_total = band_rows * map_width
    jacobian = jnp.einsum(
        "erwh,hk->ekrw", new_state, jacobian_weight, preferred_element_type=jnp.float32
    ).reshape(edge_total, 2, 12, pixel_total)
    confidence = jax.nn.softplus(
        jnp.einsum(
            "erwh,hk->ekrw", new_state, confidence_weight, preferred_element_type=jnp.float32
        )
    ).reshape(edge_total, 2, 1, pixel_total)
    normal_blocks = jnp.einsum(
        "ekap,ekbp->eab", jacobian * confidence, jacobian, precision=lax.Precision.HIGHEST
    ) / (MAPH * MAPW)
    normal_blocks = total_of_pieces(normal_blocks, "tile")
    normal_blocks = normal_blocks * in_use.astype(jnp.float32)[:, None, None]
    outgoing = jnp.concatenate(
        [
            normal_blocks[:, 6:, 6:].reshape(edge_total, 36),
            normal_blocks[:, :6, 6:].reshape(edge_total, 36),
        ],
        axis=1,
    )
    slot_blocks = jnp.einsum(
        "es,eq->sq", slot_hits.astype(jnp.float32), outgoing, precision=lax.Precision.HIGHEST
    ).reshape(owner_count, slot_depth, 72)
    incoming = lax.all_to_all(slot_blocks, "edge", split_axis=0, concat_axis=0, tiled=True).reshape(
        owner_count * slot_depth, 72
    )
    flat_target = got_target.reshape(-1)
    flat_source = got_source.reshape(-1)
    row_frames = jnp.concatenate(
        [source_global, target_global, my_index * frame_total + flat_target, flat_source]
    )
    col_frames = jnp.concatenate([edge_source, edge_source, flat_target, flat_target])
    block_list = jnp.concatenate(
        [
            normal_blocks[:, :6, :6],
            normal_blocks[:, 6:, :6],
            incoming[:, :36].reshape(-1, 6, 6),
            incoming[:, 36:].reshape(-1, 6, 6),
        ],
        axis=0,
    )
    on_diagonal = (row_frames == my_index * frame_total + col_frames).astype(jnp.float32)
    col_hits = (col_frames[:, None] == jnp.arange(frame_total)[None, :]).astype(jnp.float32)
    diagonal_part = jnp.einsum(
        "if,iq->fq",
        col_hits * on_diagonal[:, None],
        block_list.reshape(-1, 36),
        precision=lax.Precision.HIGHEST,
    )
    apart_blocks = block_list * (1.0 - on_diagonal)[:, None, None]
    spread = (apart_blocks[:, :, None, :] * col_hits[:, None, :, None]).reshape(
        -1, 6, frame_total * 6
    )
    own_rows = frame_total * owner_count * 6 // lax.axis_size("tile")
    frame_span = own_rows // 6
    row_hits = (
        row_frames[:, None]
        == lax.axis_index("tile") * own_rows // 6 + jnp.arange(frame_span)[None, :]
    ).astype(jnp.float32)
    placed = jnp.einsum("ic,ixq->cxq", row_hits, spread, precision=lax.Precision.HIGHEST)
    camera_hessian = placed.reshape(own_rows, frame_total * 6)
    return (hidden_next, camera_hessian, diagonal_part)


def solution(mesh):
    placed = (
        P("edge", "tile", None, None),
        P("edge", "tile", None, None),
        P("edge"),
        P("edge", None),
        P("edge"),
        P("edge"),
        P(),
        P(),
        P(),
        P(),
        P(),
    )
    return jax.shard_map(
        per_device,
        mesh=mesh,
        in_specs=placed,
        out_specs=(P("edge", "tile", None, None), P("tile", "edge"), P("edge", None)),
        check_vma=False,
    )
```

```python
import jax
import jax.numpy as jnp
import numpy as np
from jax import lax
from jax.experimental import pallas as pl
from jax.experimental.pallas import tpu as pltpu
from jax.sharding import PartitionSpec as P

MAPH = 48
MAPW = 64
WINDOW = 7
RADIUS = WINDOW // 2
BAND = 3
CHIP = 2 * BAND
POSE = 12
F32 = jnp.float32
BF16 = jnp.bfloat16

DOWN_TILES = [(-3, 0), (-2, 0), (-1, 0), (-1, 1), (0, 0), (0, 1), (1, 0), (1, 1), (1, 2)]
MID_TILES = [(2, 0), (2, 1), (2, 2), (3, 0), (3, 1), (3, 2)]
UP_TILES = [(4, 0), (4, 1), (4, 2), (5, 1), (5, 2), (6, 1), (6, 2), (7, 2), (8, 2)]


def window_selector():
    chosen = np.zeros((256, CHIP + 4, WINDOW * WINDOW), np.float32)

    def fill(base, tiles, rows, moved):
        for p, (row, pair) in enumerate(tiles):
            mine = row + moved
            if mine not in rows:
                continue
            for half in range(2):
                a = 2 * pair + half - row
                if abs(a) > RADIUS:
                    continue
                for d in range(WINDOW):
                    b = RADIUS - d
                    chosen[base + 64 * half + WINDOW * p + d, mine + 2, (a + RADIUS) * WINDOW + b + RADIUS] = 1.0

    fill(0, DOWN_TILES, range(-2, 2), 0)
    fill(0, MID_TILES, range(2, 4), 0)
    fill(0, UP_TILES, range(4, 8), 0)
    fill(128, UP_TILES, range(-2, 3), -CHIP)
    fill(128, DOWN_TILES, range(3, 8), CHIP)
    return chosen


def turned_order():
    turn = np.zeros((2 * MAPW, 2 * MAPW), np.float32)
    for half in range(2):
        for pixel in range(MAPW):
            turn[(64 * half + 63 - pixel + 68) % 128, 64 * half + pixel] = 1.0
    return turn


def spread_selector():
    spread = np.zeros((3, 128, 384), np.float32)
    for part, base in enumerate((0, 6, 22)):
        for y in range(6):
            spread[part, base + y, [c for c in range(144) if c % 6 == y]] = 1.0
            spread[part, base + y, [256 + c for c in range(36) if c % 6 == y]] = 1.0
    return spread


def request_kernel(owner_ref, target_ref, source_ref, out_ref, slot_ref):
    total = target_ref.shape[0]
    rows = lax.broadcasted_iota(jnp.int32, (16, 128), 0)
    lanes = lax.broadcasted_iota(jnp.int32, (16, 128), 1)
    table = jnp.zeros((16, 128), jnp.int32)
    owners = [owner_ref[e] for e in range(total)]
    for e in range(total):
        owner = owners[e]
        rank = jnp.int32(0)
        for f in range(e):
            rank = rank + jnp.where(owners[f] == owner, 1, 0)
        slot_ref[e] = owner * 2 + rank
        table = jnp.where((rows == owner) & (lanes == rank), target_ref[e], table)
        table = jnp.where((rows == owner) & (lanes == rank + 2), source_ref[e], table)
    out_ref[:, 0, :] = table


def run_all(copies):
    for c in copies:
        c.start()
    for c in copies:
        c.wait()


def pack_kernel(source_ref, features_ref, hidden_ref, keep_ref, send_ref, sems):
    half = keep_ref.shape[0]
    core = lax.axis_index("tile") % 2
    copies = []
    for n, (ref, first) in enumerate(((keep_ref, half * core), (send_ref, half * (1 - core)))):
        for e in range(half):
            edge = first + e
            copies.append(
                pltpu.make_async_copy(
                    features_ref.at[source_ref[edge]], ref.at[e, pl.ds(0, BAND)], sems.at[n, e, 0]
                )
            )
            copies.append(
                pltpu.make_async_copy(
                    hidden_ref.at[edge], ref.at[e, pl.ds(BAND, BAND)], sems.at[n, e, 1]
                )
            )
    run_all(copies)


def pick_kernel(slot_ref, maps_ref, keep_ref, send_ref, sems):
    half = send_ref.shape[0]
    core = lax.axis_index("tile") % 2
    copies = []
    for n, (ref, first) in enumerate(((send_ref, half * (1 - core)), (keep_ref, half * core))):
        for e in range(half):
            copies.append(
                pltpu.make_async_copy(maps_ref.at[slot_ref[first + e]], ref.at[e], sems.at[n, e])
            )
    run_all(copies)


def spread_columns(wide, pixel, row, value, base):
    at = slice(MAPW * row, MAPW * (row + 1))
    wide[at, base + 128 : base + 256] = value.astype(BF16)
    left = jnp.where(pixel == 0, 0.0, pltpu.roll(value, 1, 0))
    wide[at, base : base + 128] = left.astype(BF16)
    right = jnp.where(pixel == MAPW - 1, 0.0, pltpu.roll(value, MAPW - 1, 0))
    wide[at, base + 256 : base + 384] = right.astype(BF16)


def place_bands(bands, refs, e, rows, core):
    keep_ref, came_ref, ring_ref, cross_ref = refs
    for ref, band in (
        (keep_ref, 1 + core),
        (came_ref, 2 - core),
        (ring_ref, 3 * (1 - core)),
        (cross_ref, 3 * core),
    ):
        bands[pl.ds(band, 1)] = ref[e, rows][None]


def prepare_kernel(keep_ref, came_ref, ring_ref, cross_ref, gate_ref, state_ref, part_ref, bands, slabs):
    tile = lax.axis_index("tile")
    has_above = jnp.where(tile < 2, 0.0, 1.0).astype(F32)
    has_below = jnp.where(tile >= lax.axis_size("tile") - 2, 0.0, 1.0).astype(F32)
    pixel = lax.broadcasted_iota(jnp.int32, (MAPW, 128), 0)
    span = (CHIP + 2) * MAPW
    refs = (keep_ref, came_ref, ring_ref, cross_ref)
    for e in range(keep_ref.shape[0]):
        wide, rows = slabs.at[e], bands.at[e]
        place_bands(rows, refs, e, slice(BAND, CHIP), tile % 2)
        for row in range(CHIP + 4):
            state = rows[(row + 1) // BAND, (row + 1) % BAND].astype(F32)
            if row < 2:
                state = state * has_above
            if row >= 8:
                state = state * has_below
            state_ref[e, row] = state.astype(BF16)
            spread_columns(wide, pixel, row, state, 0)
        part_ref[e] = (
            jnp.dot(wide[0:span], gate_ref[0, 0:384], preferred_element_type=F32)
            + jnp.dot(wide[MAPW : MAPW + span], gate_ref[1, 0:384], preferred_element_type=F32)
            + jnp.dot(wide[2 * MAPW : 2 * MAPW + span], gate_ref[2, 0:384], preferred_element_type=F32)
        )


def corr_kernel(
    keep_ref,
    side_ref,
    ring_ref,
    cross_ref,
    kept_ref,
    came_ref,
    turn_ref,
    down_ref,
    mid_ref,
    up_ref,
    bands,
    tbuf,
):
    core = lax.axis_index("tile") % 2
    lane = lax.broadcasted_iota(jnp.int32, (MAPW, 128), 1) & 63
    pixel = lax.broadcasted_iota(jnp.int32, (MAPW, 128), 0)
    slot = (lane * 37) >> 8
    across = pixel + RADIUS - (lane - WINDOW * slot)
    inside = (across >= 0) & (across < MAPW) & (slot < 9)
    for e in range(keep_ref.shape[0]):
        place_bands(bands.at[e], (keep_ref, side_ref, ring_ref, cross_ref), e, slice(0, BAND), core)
        sources = bands[e].reshape(4 * BAND * MAPW, 128)
        tbuf[e, pl.ds(core, 1)] = kept_ref[e][None]
        tbuf[e, pl.ds(1 - core, 1)] = came_ref[e][None]
        rows = tbuf[e].reshape(CHIP * MAPW, 128)
        products = []
        for q in range(3):
            near = sources[2 * q * MAPW : (2 * q + 8) * MAPW]
            far = jnp.dot(
                turn_ref[...], rows[128 * q : 128 * (q + 1)], preferred_element_type=F32
            ).astype(BF16)
            products.append(
                lax.dot_general(near, far, (((1,), (1,)), ((), ())), preferred_element_type=F32)
            )
        for ref, tiles in ((down_ref, DOWN_TILES), (mid_ref, MID_TILES), (up_ref, UP_TILES)):
            held = jnp.zeros((MAPW, 128), F32)
            for p, (row, q) in enumerate(tiles):
                at = MAPW * (row + RADIUS - 2 * q)
                turned = pltpu.roll(
                    products[q][at : at + MAPW], WINDOW * p, 1, stride=1, stride_axis=0
                )
                held = jnp.where(slot == p, turned, held)
            ref[e] = jnp.where(inside, held * (128.0**-0.5), 0.0).astype(BF16)


def logistic(x):
    return 0.5 * jnp.tanh(0.5 * x) + 0.5


def update_kernel(
    counts_ref,
    down_ref,
    mid_ref,
    up_ref,
    above_ref,
    below_ref,
    state_ref,
    part_ref,
    window_ref,
    gate_ref,
    cand_ref,
    jac_ref,
    conf_ref,
    kept_ref,
    given_ref,
    sums_ref,
    slabs,
    rows_out,
):
    tile = lax.axis_index("tile")
    core = tile % 2
    half = state_ref.shape[0]
    has_above = jnp.where(tile < 2, 0.0, 1.0).astype(F32)
    has_below = jnp.where(tile >= lax.axis_size("tile") - 2, 0.0, 1.0).astype(F32)
    pixel = lax.broadcasted_iota(jnp.int32, (MAPW, 128), 0)
    total = jnp.zeros((16, 128), F32)
    for e in range(half):
        wide = slabs.at[e]
        used = half * core + e < counts_ref[0]
        above = (above_ref[e].astype(F32) * has_above).astype(BF16)
        below = (below_ref[e].astype(F32) * has_below).astype(BF16)
        down, mid, up = down_ref[e], mid_ref[e], up_ref[e]
        groups = (
            (down, above, 0, 4),
            (mid, above, 4, 1),
            (mid, below, 5, 1),
            (up, below, 6, 4),
        )
        for own, other, start, count in groups:
            lanes = jnp.concatenate([own, other], axis=1)
            motion = jnp.dot(
                lanes,
                window_ref[:, 128 * start : 128 * (start + count)],
                preferred_element_type=F32,
            )
            motion = jnp.maximum(motion, 0.0)
            for n in range(count):
                row = start + n
                part = motion[:, 128 * n : 128 * (n + 1)]
                if row < 2:
                    part = part * has_above
                if row >= 8:
                    part = part * has_below
                spread_columns(wide, pixel, row, part, 384)
        span = (CHIP + 2) * MAPW
        gates = part_ref[e]
        for tap in range(3):
            gates = gates + jnp.dot(
                wide[MAPW * tap : MAPW * tap + span, 384:768],
                gate_ref[tap, 384:768],
                preferred_element_type=F32,
            )
        gates = logistic(gates)
        for row in range(CHIP + 2):
            reset = gates[MAPW * row : MAPW * (row + 1), 128:256]
            spread_columns(wide, pixel, row + 1, reset * state_ref[e, row + 1].astype(F32), 0)
        span = CHIP * MAPW
        candidate = jnp.zeros((span, 128), F32)
        for tap in range(3):
            candidate = candidate + jnp.dot(
                wide[MAPW * (tap + 1) : MAPW * (tap + 1) + span],
                cand_ref[tap],
                preferred_element_type=F32,
            )
        candidate = jnp.tanh(candidate)
        update = gates[MAPW : MAPW + span, 0:128]
        old = state_ref[e, 2 : 2 + CHIP].reshape(span, 128).astype(F32)
        fresh = ((1.0 - update) * old + update * candidate).astype(BF16)
        chosen = jnp.full((span, 128), jnp.where(used, 1, 0)) == 1
        kept = jnp.where(chosen, fresh.astype(F32), old).astype(BF16)
        rows_out[e] = kept.reshape(2, BAND, MAPW, 128)
        kept_ref[e] = rows_out[e, pl.ds(core, 1)][0]
        given_ref[e] = rows_out[e, pl.ds(1 - core, 1)][0]
        jac = jnp.dot(fresh, jac_ref[...], preferred_element_type=F32)
        logit = jnp.dot(fresh, conf_ref[...], preferred_element_type=F32)
        conf = jnp.maximum(logit, 0.0) + jnp.log1p(jnp.exp(-jnp.abs(logit)))
        normal = lax.dot_general(
            (jac * conf).astype(BF16),
            jac.astype(BF16),
            (((0,), (0,)), ((), ())),
            preferred_element_type=F32,
        )
        block = normal[0:16] + pltpu.roll(normal[64:80], 64, 1)
        lane = lax.broadcasted_iota(jnp.int32, (16, 128), 1)
        block = jnp.where(lane < 16, block, 0.0)
        block = block * jnp.where(used, 1.0 / (MAPH * MAPW), 0.0).astype(F32)
        if e:
            block = pltpu.roll(block, 32 * e, 1)
        total = total + block
    for n in range(sums_ref.shape[0]):
        sums_ref[n] = total


def slots_kernel(slot_ref, parts_ref, own_ref, out_ref):
    halves = [parts_ref[h] for h in range(2)]
    for z in range(1, parts_ref.shape[0] // 2):
        for h in range(2):
            halves[h] = halves[h] + parts_ref[2 * z + h]
    out_ref[...] = jnp.zeros_like(out_ref)
    lane = lax.broadcasted_iota(jnp.int32, (16, 128), 1)
    for e in range(8):
        block = halves[e // 4]
        if e % 4:
            block = pltpu.roll(block, 128 - 32 * (e % 4), 1)
        block = jnp.where(lane < 16, block, 0.0)
        own_ref[e] = block
        slot = slot_ref[e]
        rank = slot & 1
        out_ref[slot >> 1] += pltpu.roll(block, 16 * rank, 1)


def split_dot(hits, values):
    upper = values.astype(BF16)
    lower = (values - upper.astype(F32)).astype(BF16)
    return jnp.dot(hits, upper, preferred_element_type=F32) + jnp.dot(
        hits, lower, preferred_element_type=F32
    )


def dot_split(values, hits):
    upper = values.astype(BF16)
    lower = (values - upper.astype(F32)).astype(BF16)
    return jnp.dot(upper, hits, preferred_element_type=F32) + jnp.dot(
        lower, hits, preferred_element_type=F32
    )


def place_kernel(own_ref, came_ref, spread_ref, rows_ref, cols_ref, frames_ref, within_ref, hess_ref, diag_ref):
    own = own_ref[...].reshape(128, 128)
    came = came_ref[...].reshape(256, 128)
    values = jnp.concatenate(
        [
            dot_split(own, spread_ref[0]),
            dot_split(came, spread_ref[1]),
            dot_split(came, spread_ref[2]),
        ],
        axis=0,
    )
    hess_ref[...] = split_dot(rows_ref[...], values[:, 0:144] * cols_ref[...])
    diag_ref[...] = split_dot(frames_ref[...], values[:, 256:292] * within_ref[...])


def per_device(
    features,
    hidden_state,
    edge_source,
    edge_owner,
    edge_target,
    edge_counts,
    corr_weight,
    gate_weight,
    candidate_weight,
    jacobian_weight,
    confidence_weight,
):
    edge_total = hidden_state.shape[0]
    half = edge_total // 2
    frame_total = features.shape[0]
    channels = features.shape[3]
    owner_count = lax.axis_size("edge")
    tile_count = lax.axis_size("tile")
    my_index = lax.axis_index("edge")
    tile = lax.axis_index("tile")
    core = tile % 2
    band_shape = features.shape[1:]
    smem = pl.BlockSpec(memory_space=pltpu.SMEM)
    vmem = pl.BlockSpec(memory_space=pltpu.VMEM)
    anywhere = pl.BlockSpec(memory_space=pltpu.HBM)
    beside = [(i, i ^ 1) for i in range(tile_count)]
    ring_pairs = [(i, (i + (2 if i % 2 else -2)) % tile_count) for i in range(tile_count)]
    cross_pairs = [(i, (i + (1 if i % 2 else -1)) % tile_count) for i in range(tile_count)]
    onward = [(i, (i + 2) % tile_count) for i in range(tile_count)]
    backward = [((i + 2) % tile_count, i) for i in range(tile_count)]

    requests, slot_index = pl.pallas_call(
        request_kernel,
        out_shape=(
            jax.ShapeDtypeStruct((owner_count, 1, 128), jnp.int32),
            jax.ShapeDtypeStruct((edge_total,), jnp.int32),
        ),
        in_specs=[smem, smem, smem],
        out_specs=(vmem, smem),
        name="requests",
    )(edge_owner.reshape(-1), edge_target, edge_source)
    requests, pack_source = lax.optimization_barrier((requests, edge_source))
    got = lax.all_to_all(requests, "edge", split_axis=0, concat_axis=0, tiled=True)
    keep, send = pl.pallas_call(
        pack_kernel,
        out_shape=(jax.ShapeDtypeStruct((half, CHIP) + band_shape[1:], BF16),) * 2,
        in_specs=[smem, anywhere, anywhere],
        out_specs=(vmem, vmem),
        scratch_shapes=[pltpu.SemaphoreType.DMA((2, half, 2))],
        name="pack",
    )(pack_source, features, hidden_state)
    got, keep, send = lax.optimization_barrier((got, keep, send))
    came = lax.ppermute(send, "tile", beside)
    ring = lax.ppermute(keep, "tile", ring_pairs)
    cross = lax.ppermute(send, "tile", cross_pairs)
    asked = jnp.take(features, got[:, 0, 0:2].reshape(-1), axis=0, mode="clip")
    returned = lax.all_to_all(
        asked.reshape((owner_count, 2) + band_shape), "edge", split_axis=0, concat_axis=0, tiled=True
    ).reshape((2 * owner_count,) + band_shape)
    corr_w, gate_w, cand_w = corr_weight, gate_weight, candidate_weight
    jac_w, conf_w = jacobian_weight, confidence_weight
    sources = edge_source
    window = jnp.einsum(
        "lrd,dc->lrc", jnp.asarray(window_selector(), BF16), corr_w, preferred_element_type=F32
    ).astype(BF16).reshape(256, (CHIP + 4) * 128)
    gate_w = jnp.concatenate(
        [gate_w[:, :, :channels].reshape(3, 384, 256), gate_w[:, :, channels:].reshape(3, 384, 256)],
        axis=1,
    )
    cand_w = jnp.concatenate(
        [cand_w[:, :, :channels].reshape(3, 384, 128), cand_w[:, :, channels:].reshape(3, 384, 128)],
        axis=1,
    )
    gap = jnp.zeros((channels, 64 - POSE), BF16)
    jac_w = jnp.concatenate([jac_w[:, :POSE], gap, jac_w[:, POSE:], gap], axis=1)
    conf_w = jnp.concatenate(
        [
            jnp.broadcast_to(conf_w[:, 0:1], (channels, POSE)),
            gap,
            jnp.broadcast_to(conf_w[:, 1:2], (channels, POSE)),
            gap,
        ],
        axis=1,
    )
    state_rows, gate_part = pl.pallas_call(
        prepare_kernel,
        out_shape=(
            jax.ShapeDtypeStruct((half, CHIP + 4, MAPW, 128), BF16),
            jax.ShapeDtypeStruct((half, (CHIP + 2) * MAPW, 256), F32),
        ),
        in_specs=[vmem] * 5,
        out_specs=(vmem,) * 2,
        scratch_shapes=[
            pltpu.VMEM((half, 4, BAND, MAPW, 128), BF16),
            pltpu.VMEM((half, (CHIP + 4) * MAPW, 384), BF16),
        ],
        compiler_params=pltpu.CompilerParams(vmem_limit_bytes=16 * 1024 * 1024),
        name="prepare",
    )(keep, came, ring, cross, gate_w)
    x = np.arange(16)
    asked_target, asked_source = got[:, 0, 0:2], got[:, 0, 2:4]
    other_group = jnp.arange(owner_count)[:, None] * frame_total + asked_source
    source_global = my_index * frame_total + sources
    target_global = edge_owner[:, 0] * frame_total + edge_target

    def by_row(upper, lower):
        return jnp.where(x[None, :] < 6, upper[:, None], lower[:, None]).reshape(-1)

    def each_row(value):
        return jnp.broadcast_to(value[:, None], (value.shape[0], 16)).reshape(-1)

    row_frame = jnp.concatenate(
        [by_row(source_global, target_global)]
        + [
            by_row(other_group[:, q], my_index * frame_total + asked_target[:, q])
            for q in range(2)
        ]
    )
    col_frame = jnp.concatenate([each_row(sources), each_row(asked_target[:, 0]), each_row(asked_target[:, 1])])
    stack = edge_total * 16 + 2 * owner_count * 16
    xs = np.tile(x, stack // 16)
    real = xs < POSE
    on_diagonal = row_frame == my_index * frame_total + col_frame
    own_rows = 6 * frame_total * owner_count // tile_count
    row_place = row_frame * 6 + xs % 6 - tile * own_rows
    row_place = jnp.where(real & ~on_diagonal, row_place, -1)
    diag_place = jnp.where(real & on_diagonal, col_frame, -1)
    row_hits = (jnp.arange(own_rows)[:, None] == row_place[None, :]).astype(BF16)
    diag_hits = (jnp.arange(frame_total)[:, None] == diag_place[None, :]).astype(BF16)
    col_hits = (col_frame[:, None] == (np.arange(6 * frame_total) // 6)[None, :]).astype(F32)
    within = jnp.asarray((xs[:, None] % 6 == np.arange(36)[None, :] // 6).astype(np.float32))

    kept_maps, sent_maps = pl.pallas_call(
        pick_kernel,
        out_shape=(jax.ShapeDtypeStruct((half,) + band_shape, BF16),) * 2,
        in_specs=[smem, anywhere],
        out_specs=(vmem, vmem),
        scratch_shapes=[pltpu.SemaphoreType.DMA((2, half))],
        name="pick",
    )(slot_index, returned)
    came_maps = lax.ppermute(sent_maps, "tile", beside)
    turn = jnp.asarray(turned_order(), BF16)
    down, mid, up = pl.pallas_call(
        corr_kernel,
        out_shape=(jax.ShapeDtypeStruct((half, MAPW, 128), BF16),) * 3,
        in_specs=[vmem] * 7,
        out_specs=(vmem,) * 3,
        scratch_shapes=[
            pltpu.VMEM((half, 4, BAND, MAPW, channels), BF16),
            pltpu.VMEM((half, 2, BAND, MAPW, channels), BF16),
        ],
        compiler_params=pltpu.CompilerParams(vmem_limit_bytes=16 * 1024 * 1024),
        name="windows",
    )(keep, came, ring, cross, kept_maps, came_maps, turn)
    up_came = lax.ppermute(up, "tile", onward)
    down_came = lax.ppermute(down, "tile", backward)
    kept, given, sums = pl.pallas_call(
        update_kernel,
        out_shape=(
            jax.ShapeDtypeStruct((half, BAND, MAPW, 128), BF16),
            jax.ShapeDtypeStruct((half, BAND, MAPW, 128), BF16),
            jax.ShapeDtypeStruct((tile_count, 16, 128), F32),
        ),
        in_specs=[smem] + [vmem] * 12,
        out_specs=(vmem,) * 3,
        scratch_shapes=[
            pltpu.VMEM((half, (CHIP + 4) * MAPW, 768), BF16),
            pltpu.VMEM((half, 2, BAND, MAPW, 128), BF16),
        ],
        compiler_params=pltpu.CompilerParams(vmem_limit_bytes=24 * 1024 * 1024),
        name="update",
    )(
        edge_counts,
        down,
        mid,
        up,
        up_came,
        down_came,
        state_rows,
        gate_part,
        window,
        gate_w,
        cand_w,
        jac_w,
        conf_w,
    )
    parts = lax.all_to_all(sums, "tile", split_axis=0, concat_axis=0, tiled=True)
    given_came = lax.ppermute(given, "tile", beside)
    hidden_next = jnp.where(
        core == 0,
        jnp.concatenate([kept, given_came], axis=0),
        jnp.concatenate([given_came, kept], axis=0),
    )
    own_blocks, outgoing = pl.pallas_call(
        slots_kernel,
        out_shape=(
            jax.ShapeDtypeStruct((edge_total, 16, 128), F32),
            jax.ShapeDtypeStruct((owner_count, 16, 128), F32),
        ),
        in_specs=[smem, vmem],
        out_specs=(vmem, vmem),
        name="slots",
    )(slot_index, parts)
    incoming = lax.all_to_all(outgoing, "edge", split_axis=0, concat_axis=0, tiled=True)
    camera_hessian, pose_diagonal = pl.pallas_call(
        place_kernel,
        out_shape=(
            jax.ShapeDtypeStruct((own_rows, 6 * frame_total), F32),
            jax.ShapeDtypeStruct((frame_total, 36), F32),
        ),
        in_specs=[vmem] * 7,
        out_specs=(vmem, vmem),
        name="place",
    )(own_blocks, incoming, jnp.asarray(spread_selector(), BF16), row_hits, col_hits, diag_hits, within)
    return (hidden_next, camera_hessian, pose_diagonal)


def solution(mesh):
    placed = (
        P("edge", "tile", None, None),
        P("edge", "tile", None, None),
        P("edge"),
        P("edge", None),
        P("edge"),
        P("edge"),
        P(),
        P(),
        P(),
        P(),
        P(),
    )
    return jax.shard_map(
        per_device,
        mesh=mesh,
        in_specs=placed,
        out_specs=(P("edge", "tile", None, None), P("tile", "edge"), P("edge", None)),
        check_vma=False,
    )
```

```python
import jax
import jax.numpy as jnp
import numpy as np
from jax import lax
from jax.experimental import pallas as pl
from jax.experimental.pallas import tpu as pltpu
from jax.sharding import PartitionSpec as P

MAPH = 48
MAPW = 64
WINDOW = 7
RADIUS = WINDOW // 2
BAND = 3
CHIP = 2 * BAND
POSE = 12
F32 = jnp.float32
BF16 = jnp.bfloat16

DOWN_TILES = [(-3, 0), (-2, 0), (-1, 0), (-1, 1), (0, 0), (0, 1), (1, 0), (1, 1), (1, 2)]
MID_TILES = [(2, 0), (2, 1), (2, 2), (3, 0), (3, 1), (3, 2)]
UP_TILES = [(4, 0), (4, 1), (4, 2), (5, 1), (5, 2), (6, 1), (6, 2), (7, 2), (8, 2)]


def window_selector():
    chosen = np.zeros((256, CHIP + 4, WINDOW * WINDOW), np.float32)

    def fill(base, tiles, rows, moved):
        for p, (row, pair) in enumerate(tiles):
            mine = row + moved
            if mine not in rows:
                continue
            for half in range(2):
                a = 2 * pair + half - row
                if abs(a) > RADIUS:
                    continue
                for d in range(WINDOW):
                    b = RADIUS - d
                    chosen[base + 64 * half + WINDOW * p + d, mine + 2, (a + RADIUS) * WINDOW + b + RADIUS] = 1.0

    fill(0, DOWN_TILES, range(-2, 2), 0)
    fill(0, MID_TILES, range(2, 4), 0)
    fill(0, UP_TILES, range(4, 8), 0)
    fill(128, UP_TILES, range(-2, 3), -CHIP)
    fill(128, DOWN_TILES, range(3, 8), CHIP)
    return chosen


def turned_order():
    turn = np.zeros((2 * MAPW, 2 * MAPW), np.float32)
    for half in range(2):
        for pixel in range(MAPW):
            turn[(64 * half + 63 - pixel + 68) % 128, 64 * half + pixel] = 1.0
    return turn


def request_kernel(owner_ref, target_ref, source_ref, out_ref, slot_ref):
    total = target_ref.shape[0]
    rows = lax.broadcasted_iota(jnp.int32, (16, 128), 0)
    lanes = lax.broadcasted_iota(jnp.int32, (16, 128), 1)
    table = jnp.zeros((16, 128), jnp.int32)
    owners = [owner_ref[e] for e in range(total)]
    for e in range(total):
        owner = owners[e]
        rank = jnp.int32(0)
        for f in range(e):
            rank = rank + jnp.where(owners[f] == owner, 1, 0)
        slot_ref[e] = owner * 2 + rank
        table = jnp.where((rows == owner) & (lanes == rank), target_ref[e], table)
        table = jnp.where((rows == owner) & (lanes == rank + 2), source_ref[e], table)
    out_ref[:, 0, :] = table


def run_all(copies):
    for c in copies:
        c.start()
    for c in copies:
        c.wait()


def pack_kernel(source_ref, features_ref, hidden_ref, keep_ref, send_ref, sems):
    half = keep_ref.shape[0]
    core = lax.axis_index("tile") % 2
    copies = []
    for n, (ref, first) in enumerate(((keep_ref, half * core), (send_ref, half * (1 - core)))):
        for e in range(half):
            edge = first + e
            copies.append(
                pltpu.make_async_copy(
                    features_ref.at[source_ref[edge]], ref.at[e, pl.ds(0, BAND)], sems.at[n, e, 0]
                )
            )
            copies.append(
                pltpu.make_async_copy(
                    hidden_ref.at[edge], ref.at[e, pl.ds(BAND, BAND)], sems.at[n, e, 1]
                )
            )
    run_all(copies)


def pick_kernel(slot_ref, maps_ref, keep_ref, send_ref, sems):
    half = send_ref.shape[0]
    core = lax.axis_index("tile") % 2
    copies = []
    for n, (ref, first) in enumerate(((send_ref, half * (1 - core)), (keep_ref, half * core))):
        for e in range(half):
            copies.append(
                pltpu.make_async_copy(maps_ref.at[slot_ref[first + e]], ref.at[e], sems.at[n, e])
            )
    run_all(copies)


def spread_columns(wide, pixel, row, value, base):
    at = slice(MAPW * row, MAPW * (row + 1))
    wide[at, base + 128 : base + 256] = value.astype(BF16)
    left = jnp.where(pixel == 0, 0.0, pltpu.roll(value, 1, 0))
    wide[at, base : base + 128] = left.astype(BF16)
    right = jnp.where(pixel == MAPW - 1, 0.0, pltpu.roll(value, MAPW - 1, 0))
    wide[at, base + 256 : base + 384] = right.astype(BF16)


def place_bands(bands, refs, e, rows, core):
    keep_ref, came_ref, ring_ref, cross_ref = refs
    for ref, band in (
        (keep_ref, 1 + core),
        (came_ref, 2 - core),
        (ring_ref, 3 * (1 - core)),
        (cross_ref, 3 * core),
    ):
        bands[pl.ds(band, 1)] = ref[e, rows][None]


def prepare_kernel(keep_ref, came_ref, ring_ref, cross_ref, gate_ref, state_ref, part_ref, bands, slabs):
    tile = lax.axis_index("tile")
    has_above = jnp.where(tile < 2, 0.0, 1.0).astype(F32)
    has_below = jnp.where(tile >= lax.axis_size("tile") - 2, 0.0, 1.0).astype(F32)
    pixel = lax.broadcasted_iota(jnp.int32, (MAPW, 128), 0)
    span = (CHIP + 2) * MAPW
    refs = (keep_ref, came_ref, ring_ref, cross_ref)
    for e in range(keep_ref.shape[0]):
        wide, rows = slabs.at[e], bands.at[e]
        place_bands(rows, refs, e, slice(BAND, CHIP), tile % 2)
        for row in range(CHIP + 4):
            state = rows[(row + 1) // BAND, (row + 1) % BAND].astype(F32)
            if row < 2:
                state = state * has_above
            if row >= 8:
                state = state * has_below
            state_ref[e, row] = state.astype(BF16)
            spread_columns(wide, pixel, row, state, 0)
        part_ref[e] = (
            jnp.dot(wide[0:span], gate_ref[0, 0:384], preferred_element_type=F32)
            + jnp.dot(wide[MAPW : MAPW + span], gate_ref[1, 0:384], preferred_element_type=F32)
            + jnp.dot(wide[2 * MAPW : 2 * MAPW + span], gate_ref[2, 0:384], preferred_element_type=F32)
        )


def corr_kernel(
    keep_ref,
    side_ref,
    ring_ref,
    cross_ref,
    kept_ref,
    came_ref,
    turn_ref,
    down_ref,
    mid_ref,
    up_ref,
    bands,
    tbuf,
):
    core = lax.axis_index("tile") % 2
    lane = lax.broadcasted_iota(jnp.int32, (MAPW, 128), 1) & 63
    pixel = lax.broadcasted_iota(jnp.int32, (MAPW, 128), 0)
    slot = (lane * 37) >> 8
    across = pixel + RADIUS - (lane - WINDOW * slot)
    inside = (across >= 0) & (across < MAPW) & (slot < 9)
    for e in range(kept_ref.shape[0]):
        place_bands(bands.at[e], (keep_ref, side_ref, ring_ref, cross_ref), e, slice(0, BAND), core)
        sources = bands[e].reshape(4 * BAND * MAPW, 128)
        tbuf[e, pl.ds(core, 1)] = kept_ref[e][None]
        tbuf[e, pl.ds(1 - core, 1)] = came_ref[e][None]
        rows = tbuf[e].reshape(CHIP * MAPW, 128)
        products = []
        for q in range(3):
            near = sources[2 * q * MAPW : (2 * q + 8) * MAPW]
            far = jnp.dot(
                turn_ref[...], rows[128 * q : 128 * (q + 1)], preferred_element_type=F32
            ).astype(BF16)
            products.append(
                lax.dot_general(near, far, (((1,), (1,)), ((), ())), preferred_element_type=F32)
            )
        for ref, tiles in ((down_ref, DOWN_TILES), (mid_ref, MID_TILES), (up_ref, UP_TILES)):
            held = jnp.zeros((MAPW, 128), F32)
            for p, (row, q) in enumerate(tiles):
                at = MAPW * (row + RADIUS - 2 * q)
                turned = pltpu.roll(
                    products[q][at : at + MAPW], WINDOW * p, 1, stride=1, stride_axis=0
                )
                held = jnp.where(slot == p, turned, held)
            ref[e] = jnp.where(inside, held * (128.0**-0.5), 0.0).astype(BF16)


def logistic(x):
    return 0.5 * jnp.tanh(0.5 * x) + 0.5


def update_kernel(
    counts_ref,
    down_ref,
    mid_ref,
    up_ref,
    above_ref,
    below_ref,
    state_ref,
    part_ref,
    window_ref,
    gate_ref,
    pair_ref,
    cand_ref,
    jac_ref,
    conf_ref,
    kept_ref,
    given_ref,
    sums_ref,
    slabs,
    gates_ref,
    rows_out,
):
    tile = lax.axis_index("tile")
    core = tile % 2
    half = state_ref.shape[0]
    has_above = jnp.where(tile < 2, 0.0, 1.0).astype(F32)
    has_below = jnp.where(tile >= lax.axis_size("tile") - 2, 0.0, 1.0).astype(F32)
    pixel = lax.broadcasted_iota(jnp.int32, (MAPW, 128), 0)
    wider = (CHIP + 2) * MAPW
    span = CHIP * MAPW
    blocks = []

    def motion_rows(e):
        above = (above_ref[e].astype(F32) * has_above).astype(BF16)
        below = (below_ref[e].astype(F32) * has_below).astype(BF16)
        down, mid, up = down_ref[e], mid_ref[e], up_ref[e]
        groups = (
            (down, above, 0, 4),
            (mid, above, 4, 1),
            (mid, below, 5, 1),
            (up, below, 6, 4),
        )
        for own, other, start, count in groups:
            lanes = jnp.concatenate([own, other], axis=1)
            motion = jnp.dot(
                lanes,
                window_ref[:, 128 * start : 128 * (start + count)],
                preferred_element_type=F32,
            )
            motion = jnp.maximum(motion, 0.0)
            for n in range(count):
                row = start + n
                part = motion[:, 128 * n : 128 * (n + 1)]
                if row < 2:
                    part = part * has_above
                if row >= 8:
                    part = part * has_below
                spread_columns(slabs.at[e], pixel, row, part, 384)

    def gate_rows(e):
        gates = part_ref[e]
        for tap in range(3):
            gates = gates + jnp.dot(
                slabs[e, MAPW * tap : MAPW * tap + wider, 384:768],
                gate_ref[tap, 384:768],
                preferred_element_type=F32,
            )
        gates_ref[e] = gates

    def reset_rows(e):
        for row in range(CHIP + 2):
            reset = logistic(gates_ref[e, MAPW * row : MAPW * (row + 1), 128:256])
            spread_columns(
                slabs.at[e], pixel, row + 1, reset * state_ref[e, row + 1].astype(F32), 0
            )

    def candidate_rows(e):
        two = jnp.dot(
            slabs[e, MAPW : 2 * MAPW + span], pair_ref[...], preferred_element_type=F32
        )
        third = jnp.dot(
            slabs[e, 3 * MAPW : 3 * MAPW + span], cand_ref[...], preferred_element_type=F32
        )
        candidate = jnp.tanh(two[0:span, 0:128] + two[MAPW : MAPW + span, 128:256] + third)
        used = half * core + e < counts_ref[0]
        update = logistic(gates_ref[e, MAPW : MAPW + span, 0:128])
        old = state_ref[e, 2 : 2 + CHIP].reshape(span, 128).astype(F32)
        fresh = ((1.0 - update) * old + update * candidate).astype(BF16)
        chosen = jnp.full((span, 128), jnp.where(used, 1, 0)) == 1
        kept = jnp.where(chosen, fresh.astype(F32), old).astype(BF16)
        rows_out[e] = kept.reshape(2, BAND, MAPW, 128)
        kept_ref[e] = rows_out[e, pl.ds(core, 1)][0]
        given_ref[e] = rows_out[e, pl.ds(1 - core, 1)][0]
        jac = jnp.dot(fresh, jac_ref[...], preferred_element_type=F32)
        logit = jnp.dot(fresh, conf_ref[...], preferred_element_type=F32)
        conf = jnp.maximum(logit, 0.0) + jnp.log1p(jnp.exp(-jnp.abs(logit)))
        normal = lax.dot_general(
            (jac * conf).astype(BF16),
            jac.astype(BF16),
            (((0,), (0,)), ((), ())),
            preferred_element_type=F32,
        )
        block = normal[0:16] + pltpu.roll(normal[64:80], 64, 1)
        lane = lax.broadcasted_iota(jnp.int32, (16, 128), 1)
        block = jnp.where(lane < 16, block, 0.0)
        block = block * jnp.where(used, 1.0 / (MAPH * MAPW), 0.0).astype(F32)
        if e:
            block = pltpu.roll(block, 32 * e, 1)
        blocks.append(block)

    stages = (motion_rows, gate_rows, reset_rows, candidate_rows)
    for step in range(half + len(stages) - 1):
        for n, stage in enumerate(stages):
            if 0 <= step - n < half:
                stage(step - n)
    total = sum(blocks[1:], blocks[0])
    for n in range(sums_ref.shape[0]):
        sums_ref[n] = total


def slots_kernel(slot_ref, parts_ref, own_ref, out_ref):
    halves = [parts_ref[h] for h in range(2)]
    for z in range(1, parts_ref.shape[0] // 2):
        for h in range(2):
            halves[h] = halves[h] + parts_ref[2 * z + h]
    out_ref[...] = jnp.zeros_like(out_ref)
    lane = lax.broadcasted_iota(jnp.int32, (16, 128), 1)
    for e in range(8):
        block = halves[e // 4]
        if e % 4:
            block = pltpu.roll(block, 128 - 32 * (e % 4), 1)
        block = jnp.where(lane < 16, block, 0.0)
        own_ref[e] = block
        slot = slot_ref[e]
        rank = slot & 1
        out_ref[slot >> 1] += pltpu.roll(block, 16 * rank, 1)


def tables_kernel(source_ref, owner_ref, target_ref, got_ref, rows_ref, cols_ref, frames_ref):
    me = lax.axis_index("edge")
    frames = frames_ref.shape[0]
    before = lax.axis_index("tile") * rows_ref.shape[0]
    stack = cols_ref.shape[0]
    edges = source_ref.shape[0]
    groups = got_ref.shape[0]
    lane = lax.broadcasted_iota(jnp.int32, (16, stack), 1)
    block, x = lane >> 4, lane & 15
    line = lax.broadcasted_iota(jnp.int32, (16, stack), 0)
    column = (lax.broadcasted_iota(jnp.int32, (16, cols_ref.shape[1]), 1) * 683) >> 12
    row_place = jnp.full((16, stack), -1, jnp.int32)
    diag_place = jnp.full((16, stack), -1, jnp.int32)
    for b in range(stack // 16):
        if b < edges:
            col = source_ref[b]
            upper = me * frames + col
            lower = owner_ref[b] * frames + target_ref[b]
        else:
            q, g = divmod(b - edges, groups)
            col = got_ref[g, 0, q]
            upper = g * frames + got_ref[g, 0, q + 2]
            lower = me * frames + col
        mine = me * frames + col
        for frame, start in ((upper, 0), (lower, 6)):
            here = (block == b) & (x >= start) & (x < start + 6)
            at = jnp.where(frame == mine, -stack, 6 * frame - before - start)
            row_place = jnp.where(here, x + at, row_place)
            diag_place = jnp.where(here, jnp.where(frame == mine, col, -1), diag_place)
        cols_ref[16 * b : 16 * (b + 1)] = jnp.where(column == col, 1.0, 0.0).astype(BF16)
    for n in range(rows_ref.shape[0] // 16):
        hit = jnp.where(line + 16 * n == row_place, 1.0, 0.0)
        rows_ref[16 * n : 16 * (n + 1)] = hit.astype(BF16)
    hits = [jnp.where(line + 16 * n == diag_place, 1.0, 0.0) for n in range(2)]
    frames_ref[...] = jnp.concatenate(hits, axis=0)[0:frames].astype(BF16)


def split_dot(hits, values):
    upper = values.astype(BF16)
    lower = (values - upper.astype(F32)).astype(BF16)
    return jnp.dot(hits, upper, preferred_element_type=F32) + jnp.dot(
        hits, lower, preferred_element_type=F32
    )


def dot_split(values, hits):
    upper = values.astype(BF16)
    lower = (values - upper.astype(F32)).astype(BF16)
    return jnp.dot(upper, hits, preferred_element_type=F32) + jnp.dot(
        lower, hits, preferred_element_type=F32
    )


def place_kernel(own_ref, came_ref, rows_ref, cols_ref, frames_ref, within_ref, hess_ref, diag_ref):
    own = own_ref[...].reshape(128, 128)
    came = came_ref[...].reshape(256, 128)
    lane = lax.broadcasted_iota(jnp.int32, (128, 384), 0)
    place = lax.broadcasted_iota(jnp.int32, (128, 384), 1)
    place = jnp.where(place < 256, place, place - 256)
    place = place - 6 * ((place * 683) >> 12)
    spread = [jnp.where(lane == place + base, 1.0, 0.0).astype(BF16) for base in (0, 6, 22)]
    values = jnp.concatenate(
        [dot_split(own, spread[0]), dot_split(came, spread[1]), dot_split(came, spread[2])],
        axis=0,
    )
    hess_ref[...] = split_dot(rows_ref[...], values[:, 0:144] * cols_ref[...].astype(F32))
    diag_ref[...] = split_dot(frames_ref[...], values[:, 256:292] * within_ref[...])


def per_device(
    features,
    hidden_state,
    edge_source,
    edge_owner,
    edge_target,
    edge_counts,
    corr_weight,
    gate_weight,
    candidate_weight,
    jacobian_weight,
    confidence_weight,
):
    edge_total = hidden_state.shape[0]
    half = edge_total // 2
    frame_total = features.shape[0]
    channels = features.shape[3]
    owner_count = lax.axis_size("edge")
    tile_count = lax.axis_size("tile")
    my_index = lax.axis_index("edge")
    tile = lax.axis_index("tile")
    core = tile % 2
    band_shape = features.shape[1:]
    smem = pl.BlockSpec(memory_space=pltpu.SMEM)
    vmem = pl.BlockSpec(memory_space=pltpu.VMEM)
    anywhere = pl.BlockSpec(memory_space=pltpu.HBM)
    beside = [(i, i ^ 1) for i in range(tile_count)]
    ring_pairs = [(i, (i + (2 if i % 2 else -2)) % tile_count) for i in range(tile_count)]
    cross_pairs = [(i, (i + (1 if i % 2 else -1)) % tile_count) for i in range(tile_count)]
    onward = [(i, (i + 2) % tile_count) for i in range(tile_count)]
    backward = [((i + 2) % tile_count, i) for i in range(tile_count)]

    requests, slot_index = pl.pallas_call(
        request_kernel,
        out_shape=(
            jax.ShapeDtypeStruct((owner_count, 1, 128), jnp.int32),
            jax.ShapeDtypeStruct((edge_total,), jnp.int32),
        ),
        in_specs=[smem, smem, smem],
        out_specs=(vmem, smem),
        name="requests",
    )(edge_owner.reshape(-1), edge_target, edge_source)
    requests, pack_source = lax.optimization_barrier((requests, edge_source))
    got = lax.all_to_all(requests, "edge", split_axis=0, concat_axis=0, tiled=True)
    keep, send = pl.pallas_call(
        pack_kernel,
        out_shape=(jax.ShapeDtypeStruct((half, CHIP) + band_shape[1:], BF16),) * 2,
        in_specs=[smem, anywhere, anywhere],
        out_specs=(vmem, vmem),
        scratch_shapes=[pltpu.SemaphoreType.DMA((2, half, 2))],
        name="pack",
    )(pack_source, features, hidden_state)
    got, keep, send = lax.optimization_barrier((got, keep, send))
    asked = jnp.take(features, got[:, 0, 0:2].reshape(-1), axis=0, mode="clip")
    came = lax.ppermute(send, "tile", beside)
    ring = lax.ppermute(keep, "tile", ring_pairs)
    cross = lax.ppermute(send, "tile", cross_pairs)
    corr_w, gate_w, cand_w = corr_weight, gate_weight, candidate_weight
    jac_w, conf_w = jacobian_weight, confidence_weight
    returned = lax.all_to_all(
        asked.reshape((owner_count, 2) + band_shape), "edge", split_axis=0, concat_axis=0, tiled=True
    ).reshape((2 * owner_count,) + band_shape)
    window = jnp.einsum(
        "lrd,dc->lrc", jnp.asarray(window_selector(), BF16), corr_w, preferred_element_type=F32
    ).astype(BF16).reshape(256, (CHIP + 4) * 128)
    gate_w = jnp.concatenate(
        [gate_w[:, :, :channels].reshape(3, 384, 256), gate_w[:, :, channels:].reshape(3, 384, 256)],
        axis=1,
    )
    cand_w = jnp.concatenate(
        [cand_w[:, :, :channels].reshape(3, 384, 128), cand_w[:, :, channels:].reshape(3, 384, 128)],
        axis=1,
    )
    cand_pair = jnp.concatenate([cand_w[0], cand_w[1]], axis=1)
    cand_w = cand_w[2]
    gap = jnp.zeros((channels, 64 - POSE), BF16)
    jac_w = jnp.concatenate([jac_w[:, :POSE], gap, jac_w[:, POSE:], gap], axis=1)
    conf_w = jnp.concatenate(
        [
            jnp.broadcast_to(conf_w[:, 0:1], (channels, POSE)),
            gap,
            jnp.broadcast_to(conf_w[:, 1:2], (channels, POSE)),
            gap,
        ],
        axis=1,
    )
    own_rows = 6 * frame_total * owner_count // tile_count
    stack = 16 * (edge_total + 2 * owner_count)
    row_hits, col_hits, diag_hits = pl.pallas_call(
        tables_kernel,
        out_shape=(
            jax.ShapeDtypeStruct((own_rows, stack), BF16),
            jax.ShapeDtypeStruct((stack, 6 * frame_total), BF16),
            jax.ShapeDtypeStruct((frame_total, stack), BF16),
        ),
        in_specs=[smem] * 4,
        out_specs=(vmem,) * 3,
        name="tables",
    )(edge_source, edge_owner.reshape(-1), edge_target, got)
    within = jnp.asarray(
        (np.arange(stack)[:, None] % 16 % 6 == np.arange(36)[None, :] // 6).astype(np.float32)
    )
    kept_maps, sent_maps = pl.pallas_call(
        pick_kernel,
        out_shape=(jax.ShapeDtypeStruct((half,) + band_shape, BF16),) * 2,
        in_specs=[smem, anywhere],
        out_specs=(vmem, vmem),
        scratch_shapes=[pltpu.SemaphoreType.DMA((2, half))],
        name="pick",
    )(slot_index, returned)
    kept_maps, keep_later = lax.optimization_barrier((kept_maps, keep))
    state_rows, gate_part = pl.pallas_call(
        prepare_kernel,
        out_shape=(
            jax.ShapeDtypeStruct((half, CHIP + 4, MAPW, 128), BF16),
            jax.ShapeDtypeStruct((half, (CHIP + 2) * MAPW, 256), F32),
        ),
        in_specs=[vmem] * 5,
        out_specs=(vmem,) * 2,
        scratch_shapes=[
            pltpu.VMEM((half, 4, BAND, MAPW, 128), BF16),
            pltpu.VMEM((half, (CHIP + 4) * MAPW, 384), BF16),
        ],
        compiler_params=pltpu.CompilerParams(vmem_limit_bytes=16 * 1024 * 1024),
        name="prepare",
    )(keep_later, came, ring, cross, gate_w)
    came_maps = lax.ppermute(sent_maps, "tile", beside)
    turn = jnp.asarray(turned_order(), BF16)
    down, mid, up = pl.pallas_call(
        corr_kernel,
        out_shape=(jax.ShapeDtypeStruct((half, MAPW, 128), BF16),) * 3,
        in_specs=[vmem] * 7,
        out_specs=(vmem,) * 3,
        scratch_shapes=[
            pltpu.VMEM((half, 4, BAND, MAPW, channels), BF16),
            pltpu.VMEM((half, 2, BAND, MAPW, channels), BF16),
        ],
        compiler_params=pltpu.CompilerParams(vmem_limit_bytes=16 * 1024 * 1024),
        name="windows",
    )(keep, came, ring, cross, kept_maps, came_maps, turn)
    up_came = lax.ppermute(up, "tile", onward)
    down_came = lax.ppermute(down, "tile", backward)
    kept, given, sums = pl.pallas_call(
        update_kernel,
        out_shape=(
            jax.ShapeDtypeStruct((half, BAND, MAPW, 128), BF16),
            jax.ShapeDtypeStruct((half, BAND, MAPW, 128), BF16),
            jax.ShapeDtypeStruct((tile_count, 16, 128), F32),
        ),
        in_specs=[smem] + [vmem] * 13,
        out_specs=(vmem,) * 3,
        scratch_shapes=[
            pltpu.VMEM((half, (CHIP + 4) * MAPW, 768), BF16),
            pltpu.VMEM((half, (CHIP + 2) * MAPW, 256), F32),
            pltpu.VMEM((half, 2, BAND, MAPW, 128), BF16),
        ],
        compiler_params=pltpu.CompilerParams(vmem_limit_bytes=24 * 1024 * 1024),
        name="update",
    )(
        edge_counts,
        down,
        mid,
        up,
        up_came,
        down_came,
        state_rows,
        gate_part,
        window,
        gate_w,
        cand_pair,
        cand_w,
        jac_w,
        conf_w,
    )
    parts = lax.all_to_all(sums, "tile", split_axis=0, concat_axis=0, tiled=True)
    given_came = lax.ppermute(given, "tile", beside)
    hidden_next = jnp.where(
        core == 0,
        jnp.concatenate([kept, given_came], axis=0),
        jnp.concatenate([given_came, kept], axis=0),
    )
    own_blocks, outgoing = pl.pallas_call(
        slots_kernel,
        out_shape=(
            jax.ShapeDtypeStruct((edge_total, 16, 128), F32),
            jax.ShapeDtypeStruct((owner_count, 16, 128), F32),
        ),
        in_specs=[smem, vmem],
        out_specs=(vmem, vmem),
        name="slots",
    )(slot_index, parts)
    incoming = lax.all_to_all(outgoing, "edge", split_axis=0, concat_axis=0, tiled=True)
    camera_hessian, pose_diagonal = pl.pallas_call(
        place_kernel,
        out_shape=(
            jax.ShapeDtypeStruct((own_rows, 6 * frame_total), F32),
            jax.ShapeDtypeStruct((frame_total, 36), F32),
        ),
        in_specs=[vmem] * 6,
        out_specs=(vmem, vmem),
        name="place",
    )(own_blocks, incoming, row_hits, col_hits, diag_hits, within)
    return (hidden_next, camera_hessian, pose_diagonal)


def solution(mesh):
    placed = (
        P("edge", "tile", None, None),
        P("edge", "tile", None, None),
        P("edge"),
        P("edge", None),
        P("edge"),
        P("edge"),
        P(),
        P(),
        P(),
        P(),
        P(),
    )
    return jax.shard_map(
        per_device,
        mesh=mesh,
        in_specs=placed,
        out_specs=(P("edge", "tile", None, None), P("tile", "edge"), P("edge", None)),
        check_vma=False,
    )
```

```python
import jax
import jax.numpy as jnp
import numpy as np
from jax import lax
from jax.experimental import pallas as pl
from jax.experimental.pallas import tpu as pltpu
from jax.sharding import PartitionSpec as P

MAPH = 48
MAPW = 64
WINDOW = 7
RADIUS = WINDOW // 2
BAND = 3
CHIP = 2 * BAND
POSE = 12
F32 = jnp.float32
BF16 = jnp.bfloat16

DOWN_TILES = [(-3, 0), (-2, 0), (-1, 0), (-1, 1), (0, 0), (0, 1), (1, 0), (1, 1), (1, 2)]
MID_TILES = [(2, 0), (2, 1), (2, 2), (3, 0), (3, 1), (3, 2)]
UP_TILES = [(4, 0), (4, 1), (4, 2), (5, 1), (5, 2), (6, 1), (6, 2), (7, 2), (8, 2)]


def window_selector():
    chosen = np.zeros((256, CHIP + 4, WINDOW * WINDOW), np.float32)

    def fill(base, tiles, rows, moved):
        for p, (row, pair) in enumerate(tiles):
            mine = row + moved
            if mine not in rows:
                continue
            for half in range(2):
                a = 2 * pair + half - row
                if abs(a) > RADIUS:
                    continue
                for d in range(WINDOW):
                    b = RADIUS - d
                    chosen[base + 64 * half + WINDOW * p + d, mine + 2, (a + RADIUS) * WINDOW + b + RADIUS] = 1.0

    fill(0, DOWN_TILES, range(-2, 2), 0)
    fill(0, MID_TILES, range(2, 4), 0)
    fill(0, UP_TILES, range(4, 8), 0)
    fill(128, UP_TILES, range(-2, 3), -CHIP)
    fill(128, DOWN_TILES, range(3, 8), CHIP)
    return chosen


def turned_order():
    turn = np.zeros((2 * MAPW, 2 * MAPW), np.float32)
    for half in range(2):
        for pixel in range(MAPW):
            turn[(64 * half + 63 - pixel + 68) % 128, 64 * half + pixel] = 1.0
    return turn


def request_kernel(owner_ref, target_ref, source_ref, out_ref, slot_ref):
    total = target_ref.shape[0]
    rows = lax.broadcasted_iota(jnp.int32, (16, 128), 0)
    lanes = lax.broadcasted_iota(jnp.int32, (16, 128), 1)
    table = jnp.zeros((16, 128), jnp.int32)
    owners = [owner_ref[e] for e in range(total)]
    for e in range(total):
        owner = owners[e]
        rank = jnp.int32(0)
        for f in range(e):
            rank = rank + jnp.where(owners[f] == owner, 1, 0)
        slot_ref[e] = owner * 2 + rank
        table = jnp.where((rows == owner) & (lanes == rank), target_ref[e], table)
        table = jnp.where((rows == owner) & (lanes == rank + 2), source_ref[e], table)
    out_ref[:, 0, :] = table


def run_all(copies):
    for c in copies:
        c.start()
    for c in copies:
        c.wait()


def pack_kernel(source_ref, features_ref, hidden_ref, keep_ref, send_ref, sems):
    half = keep_ref.shape[0]
    core = lax.axis_index("tile") % 2
    copies = []
    for n, (ref, first) in enumerate(((keep_ref, half * core), (send_ref, half * (1 - core)))):
        for e in range(half):
            edge = first + e
            copies.append(
                pltpu.make_async_copy(
                    features_ref.at[source_ref[edge]], ref.at[e, pl.ds(0, BAND)], sems.at[n, e, 0]
                )
            )
            copies.append(
                pltpu.make_async_copy(
                    hidden_ref.at[edge], ref.at[e, pl.ds(BAND, BAND)], sems.at[n, e, 1]
                )
            )
    run_all(copies)


def pick_kernel(slot_ref, maps_ref, keep_ref, send_ref, sems):
    half = send_ref.shape[0]
    core = lax.axis_index("tile") % 2
    copies = []
    for n, (ref, first) in enumerate(((send_ref, half * (1 - core)), (keep_ref, half * core))):
        for e in range(half):
            copies.append(
                pltpu.make_async_copy(maps_ref.at[slot_ref[first + e]], ref.at[e], sems.at[n, e])
            )
    run_all(copies)


def spread_columns(wide, pixel, row, value, base):
    at = slice(MAPW * row, MAPW * (row + 1))
    wide[at, base + 128 : base + 256] = value.astype(BF16)
    left = jnp.where(pixel == 0, 0.0, pltpu.roll(value, 1, 0))
    wide[at, base : base + 128] = left.astype(BF16)
    right = jnp.where(pixel == MAPW - 1, 0.0, pltpu.roll(value, MAPW - 1, 0))
    wide[at, base + 256 : base + 384] = right.astype(BF16)


def place_bands(bands, refs, e, core):
    keep_ref, came_ref, ring_ref, cross_ref = refs
    for ref, band in (
        (keep_ref, 1 + core),
        (came_ref, 2 - core),
        (ring_ref, 3 * (1 - core)),
        (cross_ref, 3 * core),
    ):
        bands[pl.ds(band, 1)] = ref[e][None]


def prepare_kernel(keep_ref, came_ref, ring_ref, cross_ref, gate_ref, state_ref, part_ref, bands, slabs):
    tile = lax.axis_index("tile")
    has_above = jnp.where(tile < 2, 0.0, 1.0).astype(F32)
    has_below = jnp.where(tile >= lax.axis_size("tile") - 2, 0.0, 1.0).astype(F32)
    pixel = lax.broadcasted_iota(jnp.int32, (MAPW, 128), 0)
    span = (CHIP + 2) * MAPW
    refs = (keep_ref, came_ref, ring_ref, cross_ref)
    for e in range(keep_ref.shape[0]):
        wide, rows = slabs.at[e], bands.at[e]
        place_bands(rows, refs, e, tile % 2)
        for row in range(CHIP + 4):
            state = rows[(row + 1) // BAND, (row + 1) % BAND].astype(F32)
            if row < 2:
                state = state * has_above
            if row >= 8:
                state = state * has_below
            state_ref[e, row] = state.astype(BF16)
            spread_columns(wide, pixel, row, state, 0)
        part_ref[e] = (
            jnp.dot(wide[0:span], gate_ref[0, 0:384], preferred_element_type=F32)
            + jnp.dot(wide[MAPW : MAPW + span], gate_ref[1, 0:384], preferred_element_type=F32)
            + jnp.dot(wide[2 * MAPW : 2 * MAPW + span], gate_ref[2, 0:384], preferred_element_type=F32)
        )


def corr_kernel(
    keep_ref,
    side_ref,
    ring_ref,
    cross_ref,
    kept_ref,
    came_ref,
    turn_ref,
    down_ref,
    mid_ref,
    up_ref,
    bands,
    tbuf,
):
    core = lax.axis_index("tile") % 2
    lane = lax.broadcasted_iota(jnp.int32, (MAPW, 128), 1) & 63
    pixel = lax.broadcasted_iota(jnp.int32, (MAPW, 128), 0)
    slot = (lane * 37) >> 8
    across = pixel + RADIUS - (lane - WINDOW * slot)
    inside = (across >= 0) & (across < MAPW) & (slot < 9)
    for e in range(kept_ref.shape[0]):
        place_bands(bands.at[e], (keep_ref, side_ref, ring_ref, cross_ref), e, core)
        sources = bands[e].reshape(4 * BAND * MAPW, 128)
        tbuf[e, pl.ds(core, 1)] = kept_ref[e][None]
        tbuf[e, pl.ds(1 - core, 1)] = came_ref[e][None]
        rows = tbuf[e].reshape(CHIP * MAPW, 128)
        products = []
        for q in range(3):
            near = sources[2 * q * MAPW : (2 * q + 8) * MAPW]
            far = jnp.dot(
                turn_ref[...], rows[128 * q : 128 * (q + 1)], preferred_element_type=F32
            ).astype(BF16)
            products.append(
                lax.dot_general(near, far, (((1,), (1,)), ((), ())), preferred_element_type=F32)
            )
        for ref, tiles in ((down_ref, DOWN_TILES), (mid_ref, MID_TILES), (up_ref, UP_TILES)):
            held = jnp.zeros((MAPW, 128), F32)
            for p, (row, q) in enumerate(tiles):
                at = MAPW * (row + RADIUS - 2 * q)
                turned = pltpu.roll(
                    products[q][at : at + MAPW], WINDOW * p, 1, stride=1, stride_axis=0
                )
                held = jnp.where(slot == p, turned, held)
            ref[e] = jnp.where(inside, held * (128.0**-0.5), 0.0).astype(BF16)


def logistic(x):
    return 0.5 * jnp.tanh(0.5 * x) + 0.5


def update_kernel(
    counts_ref,
    down_ref,
    mid_ref,
    up_ref,
    above_ref,
    below_ref,
    state_ref,
    part_ref,
    window_ref,
    gate_ref,
    pair_ref,
    cand_ref,
    jac_ref,
    conf_ref,
    kept_ref,
    given_ref,
    sums_ref,
    slabs,
    gates_ref,
    rows_out,
):
    tile = lax.axis_index("tile")
    core = tile % 2
    half = state_ref.shape[0]
    has_above = jnp.where(tile < 2, 0.0, 1.0).astype(F32)
    has_below = jnp.where(tile >= lax.axis_size("tile") - 2, 0.0, 1.0).astype(F32)
    pixel = lax.broadcasted_iota(jnp.int32, (MAPW, 128), 0)
    wider = (CHIP + 2) * MAPW
    span = CHIP * MAPW
    blocks = []

    def motion_rows(e):
        above = (above_ref[e].astype(F32) * has_above).astype(BF16)
        below = (below_ref[e].astype(F32) * has_below).astype(BF16)
        down, mid, up = down_ref[e], mid_ref[e], up_ref[e]
        groups = (
            (down, above, 0, 4),
            (mid, above, 4, 1),
            (mid, below, 5, 1),
            (up, below, 6, 4),
        )
        for own, other, start, count in groups:
            lanes = jnp.concatenate([own, other], axis=1)
            motion = jnp.dot(
                lanes,
                window_ref[:, 128 * start : 128 * (start + count)],
                preferred_element_type=F32,
            )
            motion = jnp.maximum(motion, 0.0)
            for n in range(count):
                row = start + n
                part = motion[:, 128 * n : 128 * (n + 1)]
                if row < 2:
                    part = part * has_above
                if row >= 8:
                    part = part * has_below
                spread_columns(slabs.at[e], pixel, row, part, 384)

    def gate_rows(e):
        gates = part_ref[e]
        for tap in range(3):
            gates = gates + jnp.dot(
                slabs[e, MAPW * tap : MAPW * tap + wider, 384:768],
                gate_ref[tap, 384:768],
                preferred_element_type=F32,
            )
        gates_ref[e] = gates

    def reset_rows(e):
        for row in range(CHIP + 2):
            reset = logistic(gates_ref[e, MAPW * row : MAPW * (row + 1), 128:256])
            spread_columns(
                slabs.at[e], pixel, row + 1, reset * state_ref[e, row + 1].astype(F32), 0
            )

    def candidate_rows(e):
        two = jnp.dot(
            slabs[e, MAPW : 2 * MAPW + span], pair_ref[...], preferred_element_type=F32
        )
        third = jnp.dot(
            slabs[e, 3 * MAPW : 3 * MAPW + span], cand_ref[...], preferred_element_type=F32
        )
        candidate = jnp.tanh(two[0:span, 0:128] + two[MAPW : MAPW + span, 128:256] + third)
        used = half * core + e < counts_ref[0]
        update = logistic(gates_ref[e, MAPW : MAPW + span, 0:128])
        old = state_ref[e, 2 : 2 + CHIP].reshape(span, 128).astype(F32)
        fresh = ((1.0 - update) * old + update * candidate).astype(BF16)
        chosen = jnp.full((span, 128), jnp.where(used, 1, 0)) == 1
        kept = jnp.where(chosen, fresh.astype(F32), old).astype(BF16)
        rows_out[e] = kept.reshape(2, BAND, MAPW, 128)
        kept_ref[e] = rows_out[e, pl.ds(core, 1)][0]
        given_ref[e] = rows_out[e, pl.ds(1 - core, 1)][0]
        jac = jnp.dot(fresh, jac_ref[...], preferred_element_type=F32)
        logit = jnp.dot(fresh, conf_ref[...], preferred_element_type=F32)
        conf = jnp.maximum(logit, 0.0) + jnp.log1p(jnp.exp(-jnp.abs(logit)))
        normal = lax.dot_general(
            (jac * conf).astype(BF16),
            jac.astype(BF16),
            (((0,), (0,)), ((), ())),
            preferred_element_type=F32,
        )
        block = normal[0:16] + pltpu.roll(normal[64:80], 64, 1)
        lane = lax.broadcasted_iota(jnp.int32, (16, 128), 1)
        block = jnp.where(lane < 16, block, 0.0)
        block = block * jnp.where(used, 1.0 / (MAPH * MAPW), 0.0).astype(F32)
        if e:
            block = pltpu.roll(block, 32 * e, 1)
        blocks.append(block)

    stages = (motion_rows, gate_rows, reset_rows, candidate_rows)
    for step in range(half + len(stages) - 1):
        for n, stage in enumerate(stages):
            if 0 <= step - n < half:
                stage(step - n)
    total = sum(blocks[1:], blocks[0])
    for n in range(sums_ref.shape[0]):
        sums_ref[n] = total


def slots_kernel(slot_ref, parts_ref, own_ref, out_ref):
    halves = [parts_ref[h] for h in range(2)]
    for z in range(1, parts_ref.shape[0] // 2):
        for h in range(2):
            halves[h] = halves[h] + parts_ref[2 * z + h]
    out_ref[...] = jnp.zeros_like(out_ref)
    lane = lax.broadcasted_iota(jnp.int32, (16, 128), 1)
    for e in range(8):
        block = halves[e // 4]
        if e % 4:
            block = pltpu.roll(block, 128 - 32 * (e % 4), 1)
        block = jnp.where(lane < 16, block, 0.0)
        own_ref[e] = block
        slot = slot_ref[e]
        rank = slot & 1
        out_ref[slot >> 1] += pltpu.roll(block, 16 * rank, 1)


def tables_kernel(source_ref, owner_ref, target_ref, got_ref, rows_ref, cols_ref, frames_ref):
    me = lax.axis_index("edge")
    frames = frames_ref.shape[0]
    before = lax.axis_index("tile") * rows_ref.shape[0]
    stack = cols_ref.shape[0]
    edges = source_ref.shape[0]
    groups = got_ref.shape[0]
    lane = lax.broadcasted_iota(jnp.int32, (16, stack), 1)
    block, x = lane >> 4, lane & 15
    line = lax.broadcasted_iota(jnp.int32, (16, stack), 0)
    column = (lax.broadcasted_iota(jnp.int32, (16, cols_ref.shape[1]), 1) * 683) >> 12
    row_place = jnp.full((16, stack), -1, jnp.int32)
    diag_place = jnp.full((16, stack), -1, jnp.int32)
    for b in range(stack // 16):
        if b < edges:
            col = source_ref[b]
            upper = me * frames + col
            lower = owner_ref[b] * frames + target_ref[b]
        else:
            q, g = divmod(b - edges, groups)
            col = got_ref[g, 0, q]
            upper = g * frames + got_ref[g, 0, q + 2]
            lower = me * frames + col
        mine = me * frames + col
        for frame, start in ((upper, 0), (lower, 6)):
            here = (block == b) & (x >= start) & (x < start + 6)
            at = jnp.where(frame == mine, -stack, 6 * frame - before - start)
            row_place = jnp.where(here, x + at, row_place)
            diag_place = jnp.where(here, jnp.where(frame == mine, col, -1), diag_place)
        cols_ref[16 * b : 16 * (b + 1)] = jnp.where(column == col, 1.0, 0.0).astype(BF16)
    for n in range(rows_ref.shape[0] // 16):
        hit = jnp.where(line + 16 * n == row_place, 1.0, 0.0)
        rows_ref[16 * n : 16 * (n + 1)] = hit.astype(BF16)
    hits = [jnp.where(line + 16 * n == diag_place, 1.0, 0.0) for n in range(2)]
    frames_ref[...] = jnp.concatenate(hits, axis=0)[0:frames].astype(BF16)


def split_dot(hits, values):
    upper = values.astype(BF16)
    lower = (values - upper.astype(F32)).astype(BF16)
    return jnp.dot(hits, upper, preferred_element_type=F32) + jnp.dot(
        hits, lower, preferred_element_type=F32
    )


def dot_split(values, hits):
    upper = values.astype(BF16)
    lower = (values - upper.astype(F32)).astype(BF16)
    return jnp.dot(upper, hits, preferred_element_type=F32) + jnp.dot(
        lower, hits, preferred_element_type=F32
    )


def place_kernel(own_ref, came_ref, rows_ref, cols_ref, frames_ref, within_ref, hess_ref, diag_ref):
    own = own_ref[...].reshape(128, 128)
    came = came_ref[...].reshape(256, 128)
    lane = lax.broadcasted_iota(jnp.int32, (128, 384), 0)
    place = lax.broadcasted_iota(jnp.int32, (128, 384), 1)
    place = jnp.where(place < 256, place, place - 256)
    place = place - 6 * ((place * 683) >> 12)
    spread = [jnp.where(lane == place + base, 1.0, 0.0).astype(BF16) for base in (0, 6, 22)]
    values = jnp.concatenate(
        [dot_split(own, spread[0]), dot_split(came, spread[1]), dot_split(came, spread[2])],
        axis=0,
    )
    hess_ref[...] = split_dot(rows_ref[...], values[:, 0:144] * cols_ref[...].astype(F32))
    diag_ref[...] = split_dot(frames_ref[...], values[:, 256:292] * within_ref[...])


def per_device(
    features,
    hidden_state,
    edge_source,
    edge_owner,
    edge_target,
    edge_counts,
    corr_weight,
    gate_weight,
    candidate_weight,
    jacobian_weight,
    confidence_weight,
):
    edge_total = hidden_state.shape[0]
    half = edge_total // 2
    frame_total = features.shape[0]
    channels = features.shape[3]
    owner_count = lax.axis_size("edge")
    tile_count = lax.axis_size("tile")
    my_index = lax.axis_index("edge")
    tile = lax.axis_index("tile")
    core = tile % 2
    band_shape = features.shape[1:]
    smem = pl.BlockSpec(memory_space=pltpu.SMEM)
    vmem = pl.BlockSpec(memory_space=pltpu.VMEM)
    anywhere = pl.BlockSpec(memory_space=pltpu.HBM)
    beside = [(i, i ^ 1) for i in range(tile_count)]
    ring_pairs = [(i, (i + (2 if i % 2 else -2)) % tile_count) for i in range(tile_count)]
    cross_pairs = [(i, (i + (1 if i % 2 else -1)) % tile_count) for i in range(tile_count)]
    onward = [(i, (i + 2) % tile_count) for i in range(tile_count)]
    backward = [((i + 2) % tile_count, i) for i in range(tile_count)]

    requests, slot_index = pl.pallas_call(
        request_kernel,
        out_shape=(
            jax.ShapeDtypeStruct((owner_count, 1, 128), jnp.int32),
            jax.ShapeDtypeStruct((edge_total,), jnp.int32),
        ),
        in_specs=[smem, smem, smem],
        out_specs=(vmem, smem),
        name="requests",
    )(edge_owner.reshape(-1), edge_target, edge_source)
    requests, pack_source = lax.optimization_barrier((requests, edge_source))
    got = lax.all_to_all(requests, "edge", split_axis=0, concat_axis=0, tiled=True)
    keep, send = pl.pallas_call(
        pack_kernel,
        out_shape=(jax.ShapeDtypeStruct((half, CHIP) + band_shape[1:], BF16),) * 2,
        in_specs=[smem, anywhere, anywhere],
        out_specs=(vmem, vmem),
        scratch_shapes=[pltpu.SemaphoreType.DMA((2, half, 2))],
        name="pack",
    )(pack_source, features, hidden_state)
    got, keep, send = lax.optimization_barrier((got, keep, send))
    asked = jnp.take(features, got[:, 0, 0:2].reshape(-1), axis=0, mode="clip")
    came = lax.ppermute(send, "tile", beside)
    ring = lax.ppermute(keep, "tile", ring_pairs)
    cross = lax.ppermute(send, "tile", cross_pairs)
    corr_w, gate_w, cand_w = corr_weight, gate_weight, candidate_weight
    jac_w, conf_w = jacobian_weight, confidence_weight
    returned = lax.all_to_all(
        asked.reshape((owner_count, 2) + band_shape), "edge", split_axis=0, concat_axis=0, tiled=True
    ).reshape((2 * owner_count,) + band_shape)
    window = jnp.einsum(
        "lrd,dc->lrc", jnp.asarray(window_selector(), BF16), corr_w, preferred_element_type=F32
    ).astype(BF16).reshape(256, (CHIP + 4) * 128)
    gate_w = jnp.concatenate(
        [gate_w[:, :, :channels].reshape(3, 384, 256), gate_w[:, :, channels:].reshape(3, 384, 256)],
        axis=1,
    )
    cand_w = jnp.concatenate(
        [cand_w[:, :, :channels].reshape(3, 384, 128), cand_w[:, :, channels:].reshape(3, 384, 128)],
        axis=1,
    )
    cand_pair = jnp.concatenate([cand_w[0], cand_w[1]], axis=1)
    cand_w = cand_w[2]
    gap = jnp.zeros((channels, 64 - POSE), BF16)
    jac_w = jnp.concatenate([jac_w[:, :POSE], gap, jac_w[:, POSE:], gap], axis=1)
    conf_w = jnp.concatenate(
        [
            jnp.broadcast_to(conf_w[:, 0:1], (channels, POSE)),
            gap,
            jnp.broadcast_to(conf_w[:, 1:2], (channels, POSE)),
            gap,
        ],
        axis=1,
    )
    own_rows = 6 * frame_total * owner_count // tile_count
    stack = 16 * (edge_total + 2 * owner_count)
    row_hits, col_hits, diag_hits = pl.pallas_call(
        tables_kernel,
        out_shape=(
            jax.ShapeDtypeStruct((own_rows, stack), BF16),
            jax.ShapeDtypeStruct((stack, 6 * frame_total), BF16),
            jax.ShapeDtypeStruct((frame_total, stack), BF16),
        ),
        in_specs=[smem] * 4,
        out_specs=(vmem,) * 3,
        name="tables",
    )(edge_source, edge_owner.reshape(-1), edge_target, got)
    within = jnp.asarray(
        (np.arange(stack)[:, None] % 16 % 6 == np.arange(36)[None, :] // 6).astype(np.float32)
    )
    kept_maps, sent_maps = pl.pallas_call(
        pick_kernel,
        out_shape=(pltpu.VMEM((half,) + band_shape, BF16),) * 2,
        in_specs=[smem, anywhere],
        out_specs=(vmem, vmem),
        scratch_shapes=[pltpu.SemaphoreType.DMA((2, half))],
        name="pick",
    )(slot_index, returned)
    kept_maps, keep_later = lax.optimization_barrier((kept_maps, keep))
    state_rows, gate_part = pl.pallas_call(
        prepare_kernel,
        out_shape=(
            jax.ShapeDtypeStruct((half, CHIP + 4, MAPW, 128), BF16),
            jax.ShapeDtypeStruct((half, (CHIP + 2) * MAPW, 256), F32),
        ),
        grid=(1,),
        in_specs=[pl.BlockSpec((half, BAND, MAPW, channels), lambda i: (0, 1, 0, 0))] * 4
        + [vmem],
        out_specs=(vmem,) * 2,
        scratch_shapes=[
            pltpu.VMEM((half, 4, BAND, MAPW, 128), BF16),
            pltpu.VMEM((half, (CHIP + 4) * MAPW, 384), BF16),
        ],
        compiler_params=pltpu.CompilerParams(vmem_limit_bytes=16 * 1024 * 1024),
        name="prepare",
    )(keep_later, came, ring, cross, gate_w)
    came_maps = lax.ppermute(sent_maps, "tile", beside)
    turn = jnp.asarray(turned_order(), BF16)
    down, mid, up = pl.pallas_call(
        corr_kernel,
        out_shape=(jax.ShapeDtypeStruct((half, MAPW, 128), BF16),) * 3,
        grid=(1,),
        in_specs=[pl.BlockSpec((half, BAND, MAPW, channels), lambda i: (0, 0, 0, 0))] * 4
        + [vmem] * 3,
        out_specs=(vmem,) * 3,
        scratch_shapes=[
            pltpu.VMEM((half, 4, BAND, MAPW, channels), BF16),
            pltpu.VMEM((half, 2, BAND, MAPW, channels), BF16),
        ],
        compiler_params=pltpu.CompilerParams(vmem_limit_bytes=16 * 1024 * 1024),
        name="windows",
    )(keep, came, ring, cross, kept_maps, came_maps, turn)
    up_came = lax.ppermute(up, "tile", onward)
    down_came = lax.ppermute(down, "tile", backward)
    kept, given, sums = pl.pallas_call(
        update_kernel,
        out_shape=(
            jax.ShapeDtypeStruct((half, BAND, MAPW, 128), BF16),
            jax.ShapeDtypeStruct((half, BAND, MAPW, 128), BF16),
            jax.ShapeDtypeStruct((tile_count, 16, 128), F32),
        ),
        in_specs=[smem] + [vmem] * 13,
        out_specs=(vmem,) * 3,
        scratch_shapes=[
            pltpu.VMEM((half, (CHIP + 4) * MAPW, 768), BF16),
            pltpu.VMEM((half, (CHIP + 2) * MAPW, 256), F32),
            pltpu.VMEM((half, 2, BAND, MAPW, 128), BF16),
        ],
        compiler_params=pltpu.CompilerParams(vmem_limit_bytes=24 * 1024 * 1024),
        name="update",
    )(
        edge_counts,
        down,
        mid,
        up,
        up_came,
        down_came,
        state_rows,
        gate_part,
        window,
        gate_w,
        cand_pair,
        cand_w,
        jac_w,
        conf_w,
    )
    parts = lax.all_to_all(sums, "tile", split_axis=0, concat_axis=0, tiled=True)
    given_came = lax.ppermute(given, "tile", beside)
    hidden_next = jnp.where(
        core == 0,
        jnp.concatenate([kept, given_came], axis=0),
        jnp.concatenate([given_came, kept], axis=0),
    )
    own_blocks, outgoing = pl.pallas_call(
        slots_kernel,
        out_shape=(
            pltpu.VMEM((edge_total, 16, 128), F32),
            jax.ShapeDtypeStruct((owner_count, 16, 128), F32),
        ),
        in_specs=[smem, vmem],
        out_specs=(vmem, vmem),
        name="slots",
    )(slot_index, parts)
    incoming = lax.all_to_all(outgoing, "edge", split_axis=0, concat_axis=0, tiled=True)
    camera_hessian, pose_diagonal = pl.pallas_call(
        place_kernel,
        out_shape=(
            jax.ShapeDtypeStruct((own_rows, 6 * frame_total), F32),
            jax.ShapeDtypeStruct((frame_total, 36), F32),
        ),
        in_specs=[vmem] * 6,
        out_specs=(vmem, vmem),
        name="place",
    )(own_blocks, incoming, row_hits, col_hits, diag_hits, within)
    return (hidden_next, camera_hessian, pose_diagonal)


def solution(mesh):
    placed = (
        P("edge", "tile", None, None),
        P("edge", "tile", None, None),
        P("edge"),
        P("edge", None),
        P("edge"),
        P("edge"),
        P(),
        P(),
        P(),
        P(),
        P(),
    )
    return jax.shard_map(
        per_device,
        mesh=mesh,
        in_specs=placed,
        out_specs=(P("edge", "tile", None, None), P("tile", "edge"), P("edge", None)),
        check_vma=False,
    )
```

```python
import jax
import jax.numpy as jnp
import numpy as np
from jax import lax
from jax.experimental import pallas as pl
from jax.experimental.pallas import tpu as pltpu
from jax.sharding import PartitionSpec as P

MAPH = 48
MAPW = 64
WINDOW = 7
RADIUS = WINDOW // 2
BAND = 3
CHIP = 2 * BAND
POSE = 12
F32 = jnp.float32
BF16 = jnp.bfloat16

DOWN_TILES = [(-3, 0), (-2, 0), (-1, 0), (-1, 1), (0, 0), (0, 1), (1, 0), (1, 1), (1, 2)]
MID_TILES = [(2, 0), (2, 1), (2, 2), (3, 0), (3, 1), (3, 2)]
UP_TILES = [(4, 0), (4, 1), (4, 2), (5, 1), (5, 2), (6, 1), (6, 2), (7, 2), (8, 2)]


def window_selector():
    chosen = np.zeros((256, CHIP + 4, WINDOW * WINDOW), np.float32)

    def fill(base, tiles, rows, moved):
        for p, (row, pair) in enumerate(tiles):
            mine = row + moved
            if mine not in rows:
                continue
            for half in range(2):
                a = 2 * pair + half - row
                if abs(a) > RADIUS:
                    continue
                for d in range(WINDOW):
                    b = RADIUS - d
                    chosen[base + 64 * half + WINDOW * p + d, mine + 2, (a + RADIUS) * WINDOW + b + RADIUS] = 1.0

    fill(0, DOWN_TILES, range(-2, 2), 0)
    fill(0, MID_TILES, range(2, 4), 0)
    fill(0, UP_TILES, range(4, 8), 0)
    fill(128, UP_TILES, range(-2, 3), -CHIP)
    fill(128, DOWN_TILES, range(3, 8), CHIP)
    return chosen


def turned_order():
    turn = np.zeros((2 * MAPW, 2 * MAPW), np.float32)
    for half in range(2):
        for pixel in range(MAPW):
            turn[(64 * half + 63 - pixel + 68) % 128, 64 * half + pixel] = 1.0
    return turn


def request_kernel(owner_ref, target_ref, source_ref, out_ref, slot_ref):
    total = target_ref.shape[0]
    rows = lax.broadcasted_iota(jnp.int32, (16, 128), 0)
    lanes = lax.broadcasted_iota(jnp.int32, (16, 128), 1)
    table = jnp.zeros((16, 128), jnp.int32)
    owners = [owner_ref[e] for e in range(total)]
    for e in range(total):
        owner = owners[e]
        rank = jnp.int32(0)
        for f in range(e):
            rank = rank + jnp.where(owners[f] == owner, 1, 0)
        slot_ref[e] = owner * 2 + rank
        table = jnp.where((rows == owner) & (lanes == rank), target_ref[e], table)
        table = jnp.where((rows == owner) & (lanes == rank + 2), source_ref[e], table)
    out_ref[:, 0, :] = table


def run_all(copies):
    for c in copies:
        c.start()
    for c in copies:
        c.wait()


def pack_kernel(source_ref, features_ref, hidden_ref, keep_ref, send_ref, sems):
    half = keep_ref.shape[0]
    core = lax.axis_index("tile") % 2
    copies = []
    for n, (ref, first) in enumerate(((keep_ref, half * core), (send_ref, half * (1 - core)))):
        for e in range(half):
            edge = first + e
            copies.append(
                pltpu.make_async_copy(
                    features_ref.at[source_ref[edge]], ref.at[e, pl.ds(0, BAND)], sems.at[n, e, 0]
                )
            )
            copies.append(
                pltpu.make_async_copy(
                    hidden_ref.at[edge], ref.at[e, pl.ds(BAND, BAND)], sems.at[n, e, 1]
                )
            )
    run_all(copies)


def pick_kernel(slot_ref, maps_ref, keep_ref, send_ref, sems):
    half = send_ref.shape[0]
    core = lax.axis_index("tile") % 2
    copies = []
    for n, (ref, first) in enumerate(((send_ref, half * (1 - core)), (keep_ref, half * core))):
        for e in range(half):
            copies.append(
                pltpu.make_async_copy(maps_ref.at[slot_ref[first + e]], ref.at[e], sems.at[n, e])
            )
    run_all(copies)


def spread_columns(wide, pixel, row, value, base):
    at = slice(MAPW * row, MAPW * (row + 1))
    wide[at, base + 128 : base + 256] = value.astype(BF16)
    left = jnp.where(pixel == 0, 0.0, pltpu.roll(value, 1, 0))
    wide[at, base : base + 128] = left.astype(BF16)
    right = jnp.where(pixel == MAPW - 1, 0.0, pltpu.roll(value, MAPW - 1, 0))
    wide[at, base + 256 : base + 384] = right.astype(BF16)


def place_bands(bands, refs, e, core):
    keep_ref, came_ref, ring_ref, cross_ref = refs
    for ref, band in (
        (keep_ref, 1 + core),
        (came_ref, 2 - core),
        (ring_ref, 3 * (1 - core)),
        (cross_ref, 3 * core),
    ):
        bands[pl.ds(band, 1)] = ref[e][None]


def prepare_kernel(keep_ref, came_ref, ring_ref, cross_ref, gate_ref, state_ref, part_ref, bands, slabs):
    tile = lax.axis_index("tile")
    has_above = jnp.where(tile < 2, 0.0, 1.0).astype(F32)
    has_below = jnp.where(tile >= lax.axis_size("tile") - 2, 0.0, 1.0).astype(F32)
    pixel = lax.broadcasted_iota(jnp.int32, (MAPW, 128), 0)
    span = (CHIP + 2) * MAPW
    refs = (keep_ref, came_ref, ring_ref, cross_ref)
    for e in range(keep_ref.shape[0]):
        wide, rows = slabs.at[e], bands.at[e]
        place_bands(rows, refs, e, tile % 2)
        for row in range(CHIP + 4):
            state = rows[(row + 1) // BAND, (row + 1) % BAND].astype(F32)
            if row < 2:
                state = state * has_above
            if row >= 8:
                state = state * has_below
            state_ref[e, row] = state.astype(BF16)
            spread_columns(wide, pixel, row, state, 0)
        part_ref[e] = (
            jnp.dot(wide[0:span], gate_ref[0, 0:384], preferred_element_type=F32)
            + jnp.dot(wide[MAPW : MAPW + span], gate_ref[1, 0:384], preferred_element_type=F32)
            + jnp.dot(wide[2 * MAPW : 2 * MAPW + span], gate_ref[2, 0:384], preferred_element_type=F32)
        )


def corr_kernel(
    keep_ref,
    side_ref,
    ring_ref,
    cross_ref,
    kept_ref,
    came_ref,
    turn_ref,
    down_ref,
    mid_ref,
    up_ref,
    bands,
    tbuf,
):
    core = lax.axis_index("tile") % 2
    lane = lax.broadcasted_iota(jnp.int32, (MAPW, 128), 1) & 63
    pixel = lax.broadcasted_iota(jnp.int32, (MAPW, 128), 0)
    slot = (lane * 37) >> 8
    across = pixel + RADIUS - (lane - WINDOW * slot)
    inside = (across >= 0) & (across < MAPW) & (slot < 9)
    for e in range(kept_ref.shape[0]):
        place_bands(bands.at[e], (keep_ref, side_ref, ring_ref, cross_ref), e, core)
        sources = bands[e].reshape(4 * BAND * MAPW, 128)
        tbuf[e, pl.ds(core, 1)] = kept_ref[e][None]
        tbuf[e, pl.ds(1 - core, 1)] = came_ref[e][None]
        rows = tbuf[e].reshape(CHIP * MAPW, 128)
        products = []
        for q in range(3):
            near = sources[2 * q * MAPW : (2 * q + 8) * MAPW]
            far = jnp.dot(
                turn_ref[...], rows[128 * q : 128 * (q + 1)], preferred_element_type=F32
            ).astype(BF16)
            products.append(
                lax.dot_general(near, far, (((1,), (1,)), ((), ())), preferred_element_type=F32)
            )
        for ref, tiles in ((down_ref, DOWN_TILES), (mid_ref, MID_TILES), (up_ref, UP_TILES)):
            held = jnp.zeros((MAPW, 128), F32)
            for p, (row, q) in enumerate(tiles):
                at = MAPW * (row + RADIUS - 2 * q)
                turned = pltpu.roll(
                    products[q][at : at + MAPW], WINDOW * p, 1, stride=1, stride_axis=0
                )
                held = jnp.where(slot == p, turned, held)
            ref[e] = jnp.where(inside, held * (128.0**-0.5), 0.0).astype(BF16)


def logistic(x):
    return 0.5 * jnp.tanh(0.5 * x) + 0.5


def update_kernel(
    counts_ref,
    down_ref,
    mid_ref,
    up_ref,
    above_ref,
    below_ref,
    state_ref,
    part_ref,
    window_ref,
    gate_ref,
    pair_ref,
    cand_ref,
    jac_ref,
    head_ref,
    kept_ref,
    given_ref,
    sums_ref,
    slabs,
    gates_ref,
    rows_out,
):
    tile = lax.axis_index("tile")
    core = tile % 2
    half = state_ref.shape[0]
    has_above = jnp.where(tile < 2, 0.0, 1.0).astype(F32)
    has_below = jnp.where(tile >= lax.axis_size("tile") - 2, 0.0, 1.0).astype(F32)
    pixel = lax.broadcasted_iota(jnp.int32, (MAPW, 128), 0)
    wider = (CHIP + 2) * MAPW
    span = CHIP * MAPW
    blocks = []

    def motion_rows(e):
        above = (above_ref[e].astype(F32) * has_above).astype(BF16)
        below = (below_ref[e].astype(F32) * has_below).astype(BF16)
        down, mid, up = down_ref[e], mid_ref[e], up_ref[e]
        groups = (
            (down, above, 0, 4),
            (mid, above, 4, 1),
            (mid, below, 5, 1),
            (up, below, 6, 4),
        )
        for own, other, start, count in groups:
            lanes = jnp.concatenate([own, other], axis=1)
            motion = jnp.dot(
                lanes,
                window_ref[:, 128 * start : 128 * (start + count)],
                preferred_element_type=F32,
            )
            motion = jnp.maximum(motion, 0.0)
            for n in range(count):
                row = start + n
                part = motion[:, 128 * n : 128 * (n + 1)]
                if row < 2:
                    part = part * has_above
                if row >= 8:
                    part = part * has_below
                spread_columns(slabs.at[e], pixel, row, part, 384)

    def gate_rows(e):
        gates = part_ref[e]
        for tap in range(3):
            gates = gates + jnp.dot(
                slabs[e, MAPW * tap : MAPW * tap + wider, 384:768],
                gate_ref[tap, 384:768],
                preferred_element_type=F32,
            )
        gates_ref[e] = gates

    def reset_rows(e):
        for row in range(CHIP + 2):
            reset = logistic(gates_ref[e, MAPW * row : MAPW * (row + 1), 128:256])
            spread_columns(
                slabs.at[e], pixel, row + 1, reset * state_ref[e, row + 1].astype(F32), 0
            )

    def candidate_rows(e):
        two = jnp.dot(
            slabs[e, MAPW : 2 * MAPW + span], pair_ref[...], preferred_element_type=F32
        )
        third = jnp.dot(
            slabs[e, 3 * MAPW : 3 * MAPW + span], cand_ref[...], preferred_element_type=F32
        )
        candidate = jnp.tanh(two[0:span, 0:128] + two[MAPW : MAPW + span, 128:256] + third)
        used = half * core + e < counts_ref[0]
        update = logistic(gates_ref[e, MAPW : MAPW + span, 0:128])
        old = state_ref[e, 2 : 2 + CHIP].reshape(span, 128).astype(F32)
        fresh = ((1.0 - update) * old + update * candidate).astype(BF16)
        chosen = jnp.full((span, 128), jnp.where(used, 1, 0)) == 1
        kept = jnp.where(chosen, fresh.astype(F32), old).astype(BF16)
        rows_out[e] = kept.reshape(2, BAND, MAPW, 128)
        kept_ref[e] = rows_out[e, pl.ds(core, 1)][0]
        given_ref[e] = rows_out[e, pl.ds(1 - core, 1)][0]
        jac = jnp.dot(fresh, jac_ref[...], preferred_element_type=F32)
        turned = lax.dot_general(
            head_ref[...], fresh, (((1,), (1,)), ((), ())), preferred_element_type=F32
        )
        logit = turned[32:64]
        conf = jnp.maximum(logit, 0.0) + jnp.log1p(jnp.exp(-jnp.abs(logit)))
        normal = jnp.dot(
            (turned[0:32] * conf).astype(BF16), jac.astype(BF16), preferred_element_type=F32
        )
        block = normal[0:16] + pltpu.roll(normal[16:32], 64, 1)
        lane = lax.broadcasted_iota(jnp.int32, (16, 128), 1)
        block = jnp.where(lane < 16, block, 0.0)
        block = block * jnp.where(used, 1.0 / (MAPH * MAPW), 0.0).astype(F32)
        if e:
            block = pltpu.roll(block, 32 * e, 1)
        blocks.append(block)

    stages = (motion_rows, gate_rows, reset_rows, candidate_rows)
    for step in range(half + len(stages) - 1):
        for n, stage in enumerate(stages):
            if 0 <= step - n < half:
                stage(step - n)
    total = sum(blocks[1:], blocks[0])
    for n in range(sums_ref.shape[0]):
        sums_ref[n] = total


def slots_kernel(slot_ref, parts_ref, own_ref, out_ref):
    halves = [parts_ref[h] for h in range(2)]
    for z in range(1, parts_ref.shape[0] // 2):
        for h in range(2):
            halves[h] = halves[h] + parts_ref[2 * z + h]
    out_ref[...] = jnp.zeros_like(out_ref)
    lane = lax.broadcasted_iota(jnp.int32, (16, 128), 1)
    for e in range(8):
        block = halves[e // 4]
        if e % 4:
            block = pltpu.roll(block, 128 - 32 * (e % 4), 1)
        block = jnp.where(lane < 16, block, 0.0)
        own_ref[e] = block
        slot = slot_ref[e]
        rank = slot & 1
        out_ref[slot >> 1] += pltpu.roll(block, 16 * rank, 1)


def tables_kernel(source_ref, owner_ref, target_ref, got_ref, rows_ref, cols_ref, frames_ref):
    me = lax.axis_index("edge")
    frames = frames_ref.shape[0]
    before = lax.axis_index("tile") * rows_ref.shape[0]
    stack = cols_ref.shape[0]
    edges = source_ref.shape[0]
    groups = got_ref.shape[0]
    lane = lax.broadcasted_iota(jnp.int32, (16, stack), 1)
    block, x = lane >> 4, lane & 15
    line = lax.broadcasted_iota(jnp.int32, (16, stack), 0)
    column = (lax.broadcasted_iota(jnp.int32, (16, cols_ref.shape[1]), 1) * 683) >> 12
    row_place = jnp.full((16, stack), -1, jnp.int32)
    diag_place = jnp.full((16, stack), -1, jnp.int32)
    for b in range(stack // 16):
        if b < edges:
            col = source_ref[b]
            upper = me * frames + col
            lower = owner_ref[b] * frames + target_ref[b]
        else:
            q, g = divmod(b - edges, groups)
            col = got_ref[g, 0, q]
            upper = g * frames + got_ref[g, 0, q + 2]
            lower = me * frames + col
        mine = me * frames + col
        for frame, start in ((upper, 0), (lower, 6)):
            here = (block == b) & (x >= start) & (x < start + 6)
            at = jnp.where(frame == mine, -stack, 6 * frame - before - start)
            row_place = jnp.where(here, x + at, row_place)
            diag_place = jnp.where(here, jnp.where(frame == mine, col, -1), diag_place)
        cols_ref[16 * b : 16 * (b + 1)] = jnp.where(column == col, 1.0, 0.0).astype(BF16)
    for n in range(rows_ref.shape[0] // 16):
        hit = jnp.where(line + 16 * n == row_place, 1.0, 0.0)
        rows_ref[16 * n : 16 * (n + 1)] = hit.astype(BF16)
    hits = [jnp.where(line + 16 * n == diag_place, 1.0, 0.0) for n in range(2)]
    frames_ref[...] = jnp.concatenate(hits, axis=0)[0:frames].astype(BF16)


def split_dot(hits, values):
    upper = values.astype(BF16)
    lower = (values - upper.astype(F32)).astype(BF16)
    return jnp.dot(hits, upper, preferred_element_type=F32) + jnp.dot(
        hits, lower, preferred_element_type=F32
    )


def dot_split(values, hits):
    upper = values.astype(BF16)
    lower = (values - upper.astype(F32)).astype(BF16)
    return jnp.dot(upper, hits, preferred_element_type=F32) + jnp.dot(
        lower, hits, preferred_element_type=F32
    )


def place_kernel(own_ref, came_ref, rows_ref, cols_ref, frames_ref, within_ref, hess_ref, diag_ref):
    own = own_ref[...].reshape(128, 128)
    came = came_ref[...].reshape(256, 128)
    lane = lax.broadcasted_iota(jnp.int32, (128, 384), 0)
    place = lax.broadcasted_iota(jnp.int32, (128, 384), 1)
    place = jnp.where(place < 256, place, place - 256)
    place = place - 6 * ((place * 683) >> 12)
    spread = [jnp.where(lane == place + base, 1.0, 0.0).astype(BF16) for base in (0, 6, 22)]
    values = jnp.concatenate(
        [dot_split(own, spread[0]), dot_split(came, spread[1]), dot_split(came, spread[2])],
        axis=0,
    )
    hess_ref[...] = split_dot(rows_ref[...], values[:, 0:144] * cols_ref[...].astype(F32))
    diag_ref[...] = split_dot(frames_ref[...], values[:, 256:292] * within_ref[...])


def per_device(
    features,
    hidden_state,
    edge_source,
    edge_owner,
    edge_target,
    edge_counts,
    corr_weight,
    gate_weight,
    candidate_weight,
    jacobian_weight,
    confidence_weight,
):
    edge_total = hidden_state.shape[0]
    half = edge_total // 2
    frame_total = features.shape[0]
    channels = features.shape[3]
    owner_count = lax.axis_size("edge")
    tile_count = lax.axis_size("tile")
    my_index = lax.axis_index("edge")
    tile = lax.axis_index("tile")
    core = tile % 2
    band_shape = features.shape[1:]
    smem = pl.BlockSpec(memory_space=pltpu.SMEM)
    vmem = pl.BlockSpec(memory_space=pltpu.VMEM)
    anywhere = pl.BlockSpec(memory_space=pltpu.HBM)
    beside = [(i, i ^ 1) for i in range(tile_count)]
    ring_pairs = [(i, (i + (2 if i % 2 else -2)) % tile_count) for i in range(tile_count)]
    cross_pairs = [(i, (i + (1 if i % 2 else -1)) % tile_count) for i in range(tile_count)]
    onward = [(i, (i + 2) % tile_count) for i in range(tile_count)]
    backward = [((i + 2) % tile_count, i) for i in range(tile_count)]

    requests, slot_index = pl.pallas_call(
        request_kernel,
        out_shape=(
            jax.ShapeDtypeStruct((owner_count, 1, 128), jnp.int32),
            jax.ShapeDtypeStruct((edge_total,), jnp.int32),
        ),
        in_specs=[smem, smem, smem],
        out_specs=(vmem, smem),
        name="requests",
    )(edge_owner.reshape(-1), edge_target, edge_source)
    requests, pack_source = lax.optimization_barrier((requests, edge_source))
    got = lax.all_to_all(requests, "edge", split_axis=0, concat_axis=0, tiled=True)
    keep, send = pl.pallas_call(
        pack_kernel,
        out_shape=(jax.ShapeDtypeStruct((half, CHIP) + band_shape[1:], BF16),) * 2,
        in_specs=[smem, anywhere, anywhere],
        out_specs=(vmem, vmem),
        scratch_shapes=[pltpu.SemaphoreType.DMA((2, half, 2))],
        name="pack",
    )(pack_source, features, hidden_state)
    got, keep, send = lax.optimization_barrier((got, keep, send))
    asked = jnp.take(features, got[:, 0, 0:2].reshape(-1), axis=0, mode="clip")
    came = lax.ppermute(send, "tile", beside)
    ring = lax.ppermute(keep, "tile", ring_pairs)
    cross = lax.ppermute(send, "tile", cross_pairs)
    corr_w, gate_w, cand_w = corr_weight, gate_weight, candidate_weight
    jac_w, conf_w = jacobian_weight, confidence_weight
    returned = lax.all_to_all(
        asked.reshape((owner_count, 2) + band_shape), "edge", split_axis=0, concat_axis=0, tiled=True
    ).reshape((2 * owner_count,) + band_shape)
    window = jnp.einsum(
        "lrd,dc->lrc", jnp.asarray(window_selector(), BF16), corr_w, preferred_element_type=F32
    ).astype(BF16).reshape(256, (CHIP + 4) * 128)
    gate_w = jnp.concatenate(
        [gate_w[:, :, :channels].reshape(3, 384, 256), gate_w[:, :, channels:].reshape(3, 384, 256)],
        axis=1,
    )
    cand_w = jnp.concatenate(
        [cand_w[:, :, :channels].reshape(3, 384, 128), cand_w[:, :, channels:].reshape(3, 384, 128)],
        axis=1,
    )
    cand_pair = jnp.concatenate([cand_w[0], cand_w[1]], axis=1)
    cand_w = cand_w[2]
    gap = jnp.zeros((channels, 64 - POSE), BF16)
    short = jnp.zeros((channels, 16 - POSE), BF16)
    head_w = jnp.concatenate(
        [
            jac_w[:, :POSE],
            short,
            jac_w[:, POSE:],
            short,
            jnp.broadcast_to(conf_w[:, 0:1], (channels, 16)),
            jnp.broadcast_to(conf_w[:, 1:2], (channels, 16)),
        ],
        axis=1,
    ).T
    jac_w = jnp.concatenate([jac_w[:, :POSE], gap, jac_w[:, POSE:], gap], axis=1)
    own_rows = 6 * frame_total * owner_count // tile_count
    stack = 16 * (edge_total + 2 * owner_count)
    row_hits, col_hits, diag_hits = pl.pallas_call(
        tables_kernel,
        out_shape=(
            jax.ShapeDtypeStruct((own_rows, stack), BF16),
            jax.ShapeDtypeStruct((stack, 6 * frame_total), BF16),
            jax.ShapeDtypeStruct((frame_total, stack), BF16),
        ),
        in_specs=[smem] * 4,
        out_specs=(vmem,) * 3,
        name="tables",
    )(edge_source, edge_owner.reshape(-1), edge_target, got)
    within = jnp.asarray(
        (np.arange(stack)[:, None] % 16 % 6 == np.arange(36)[None, :] // 6).astype(np.float32)
    )
    kept_maps, sent_maps = pl.pallas_call(
        pick_kernel,
        out_shape=(pltpu.VMEM((half,) + band_shape, BF16),) * 2,
        in_specs=[smem, anywhere],
        out_specs=(vmem, vmem),
        scratch_shapes=[pltpu.SemaphoreType.DMA((2, half))],
        name="pick",
    )(slot_index, returned)
    kept_maps, keep_later = lax.optimization_barrier((kept_maps, keep))
    state_rows, gate_part = pl.pallas_call(
        prepare_kernel,
        out_shape=(
            jax.ShapeDtypeStruct((half, CHIP + 4, MAPW, 128), BF16),
            jax.ShapeDtypeStruct((half, (CHIP + 2) * MAPW, 256), F32),
        ),
        grid=(1,),
        in_specs=[pl.BlockSpec((half, BAND, MAPW, channels), lambda i: (0, 1, 0, 0))] * 4
        + [vmem],
        out_specs=(vmem,) * 2,
        scratch_shapes=[
            pltpu.VMEM((half, 4, BAND, MAPW, 128), BF16),
            pltpu.VMEM((half, (CHIP + 4) * MAPW, 384), BF16),
        ],
        compiler_params=pltpu.CompilerParams(vmem_limit_bytes=16 * 1024 * 1024),
        name="prepare",
    )(keep_later, came, ring, cross, gate_w)
    came_maps = lax.ppermute(sent_maps, "tile", beside)
    turn = jnp.asarray(turned_order(), BF16)
    down, mid, up = pl.pallas_call(
        corr_kernel,
        out_shape=(jax.ShapeDtypeStruct((half, MAPW, 128), BF16),) * 3,
        grid=(1,),
        in_specs=[pl.BlockSpec((half, BAND, MAPW, channels), lambda i: (0, 0, 0, 0))] * 4
        + [vmem] * 3,
        out_specs=(vmem,) * 3,
        scratch_shapes=[
            pltpu.VMEM((half, 4, BAND, MAPW, channels), BF16),
            pltpu.VMEM((half, 2, BAND, MAPW, channels), BF16),
        ],
        compiler_params=pltpu.CompilerParams(vmem_limit_bytes=16 * 1024 * 1024),
        name="windows",
    )(keep, came, ring, cross, kept_maps, came_maps, turn)
    up_came = lax.ppermute(up, "tile", onward)
    down_came = lax.ppermute(down, "tile", backward)
    kept, given, sums = pl.pallas_call(
        update_kernel,
        out_shape=(
            jax.ShapeDtypeStruct((half, BAND, MAPW, 128), BF16),
            jax.ShapeDtypeStruct((half, BAND, MAPW, 128), BF16),
            jax.ShapeDtypeStruct((tile_count, 16, 128), F32),
        ),
        in_specs=[smem] + [vmem] * 13,
        out_specs=(vmem,) * 3,
        scratch_shapes=[
            pltpu.VMEM((half, (CHIP + 4) * MAPW, 768), BF16),
            pltpu.VMEM((half, (CHIP + 2) * MAPW, 256), F32),
            pltpu.VMEM((half, 2, BAND, MAPW, 128), BF16),
        ],
        compiler_params=pltpu.CompilerParams(vmem_limit_bytes=24 * 1024 * 1024),
        name="update",
    )(
        edge_counts,
        down,
        mid,
        up,
        up_came,
        down_came,
        state_rows,
        gate_part,
        window,
        gate_w,
        cand_pair,
        cand_w,
        jac_w,
        head_w,
    )
    parts = lax.all_to_all(sums, "tile", split_axis=0, concat_axis=0, tiled=True)
    given_came = lax.ppermute(given, "tile", beside)
    hidden_next = jnp.where(
        core == 0,
        jnp.concatenate([kept, given_came], axis=0),
        jnp.concatenate([given_came, kept], axis=0),
    )
    own_blocks, outgoing = pl.pallas_call(
        slots_kernel,
        out_shape=(
            pltpu.VMEM((edge_total, 16, 128), F32),
            jax.ShapeDtypeStruct((owner_count, 16, 128), F32),
        ),
        in_specs=[smem, vmem],
        out_specs=(vmem, vmem),
        name="slots",
    )(slot_index, parts)
    incoming = lax.all_to_all(outgoing, "edge", split_axis=0, concat_axis=0, tiled=True)
    camera_hessian, pose_diagonal = pl.pallas_call(
        place_kernel,
        out_shape=(
            jax.ShapeDtypeStruct((own_rows, 6 * frame_total), F32),
            jax.ShapeDtypeStruct((frame_total, 36), F32),
        ),
        in_specs=[vmem] * 6,
        out_specs=(vmem, vmem),
        name="place",
    )(own_blocks, incoming, row_hits, col_hits, diag_hits, within)
    return (hidden_next, camera_hessian, pose_diagonal)


def solution(mesh):
    placed = (
        P("edge", "tile", None, None),
        P("edge", "tile", None, None),
        P("edge"),
        P("edge", None),
        P("edge"),
        P("edge"),
        P(),
        P(),
        P(),
        P(),
        P(),
    )
    return jax.shard_map(
        per_device,
        mesh=mesh,
        in_specs=placed,
        out_specs=(P("edge", "tile", None, None), P("tile", "edge"), P("edge", None)),
        check_vma=False,
    )
```
